32 devices in a mesh: ctx: 8 (over z, x), head: 4 (over y, core).
Axes of the slice: x: 2, y: 2, z: 4, core: 2. Of those that a mesh axis runs over, the one named last changes fastest.
Arguments:
- query_vectors: bfloat16 [3072, 4096], P('ctx', 'head'), may hold values from -6 to 6
- key_vectors: bfloat16 [3072, 4096], P('ctx', 'head'), may hold values from -11 to 11
- value_vectors: bfloat16 [3072, 4096], P('ctx', 'head'), may hold values from -6 to 6
- log_decay: float32 [3072, 4096], P('ctx', 'head'), may hold values from -0.7 to 0, as said below
- write_rate: float32 [3072, 32], P('ctx', 'head'), may hold values from 0 to 1
- out_gate: bfloat16 [3072, 4096], P('ctx', 'head'), may hold values from -6 to 6
- norm_gain: float32 [128], replicated, may hold values from 0.25 to 1.75
- out_weight: bfloat16 [4096, 2304], P('head'), may hold values from -0.09375 to 0.09375
Outputs:
- mixed: bfloat16 [3072, 2304], P(('ctx', 'head'))
The draws below stay inside these ranges and needn't reach their ends.
Inputs may be any that keep to these rules, and one draw needn't show every extreme that they name: `log_decay`: every decay lies strictly below 1.
All inputs are finite; a program needn't handle non-finite values.
Results may differ from the reference program's by a relative error of at most 0.014.
Values may be sent and summed in bfloat16 or wider, within the bound.
No kernel may reach another device: no remote copies, remote signals or barrier semaphores. Data moves between devices by JAX's collectives and lax.ppermute only.
A program may use at most 128 MiB of HBM per device.

```python
import math
import jax
import jax.numpy as jnp
from jax import lax

D = 2304
HEAD_TOTAL = 32
HEAD_SIZE = 128
TOK_DEV = 384
TOKEN_TOTAL = 3072
HDK = 4096
N_HEAD = 4


def head_kinds(key):
    slow_share = 0.5
    return jax.random.uniform(jax.random.fold_in(key, 5), (HEAD_TOTAL,), jnp.float32) < slow_share


def draw_key_vectors(key, part):
    sequence_lanes = jax.random.split(jax.random.fold_in(key, 17), 3)
    latent_width = HEAD_SIZE // 4
    basis_signs = 2 * jax.random.randint(sequence_lanes[0], (HEAD_TOTAL, latent_width, HEAD_SIZE), 0, 2) - 1
    latent_coeffs = jax.random.randint(sequence_lanes[1], (TOKEN_TOTAL, HEAD_TOTAL, latent_width), -8, 9)
    latent_sum = jnp.einsum('tha,hac->thc', latent_coeffs, basis_signs)
    latent_part = latent_sum.astype(jnp.float32) * (1.0 / math.sqrt(24.0 * latent_width))
    own_part = jnp.clip(jax.random.normal(sequence_lanes[2], (TOKEN_TOTAL, HEAD_TOTAL, HEAD_SIZE), jnp.float32), -6.0, 6.0)
    mixed_keys = math.sqrt(0.5) * own_part + math.sqrt(0.5) * latent_part
    return mixed_keys.reshape(TOKEN_TOTAL, HEAD_TOTAL * HEAD_SIZE).astype(jnp.bfloat16)


def draw_log_decay(key, part):
    slow_heads = head_kinds(key)
    sequence_lanes = jax.random.split(jax.random.fold_in(key, 11), 6)
    fast_rates = jnp.exp(jax.random.uniform(sequence_lanes[0], (HEAD_TOTAL, HEAD_SIZE), jnp.float32, math.log(1.0 / 60.0), math.log(1.0 / 20.0)))
    gentle_rates = jax.random.uniform(sequence_lanes[1], (HEAD_TOTAL, HEAD_SIZE), jnp.float32, 0.02, 0.25) / TOKEN_TOTAL
    base_rates = jnp.where(slow_heads[:, None], gentle_rates, fast_rates).reshape(HEAD_TOTAL * HEAD_SIZE)
    block_total = TOKEN_TOTAL // TOK_DEV
    device_spread = jnp.exp(jax.random.uniform(sequence_lanes[2], (block_total, 1, HEAD_TOTAL * HEAD_SIZE), jnp.float32, math.log(0.5), math.log(2.0)))
    roughness = jax.random.uniform(sequence_lanes[3], (block_total, TOK_DEV, HEAD_TOTAL * HEAD_SIZE), jnp.float32, 0.5, 1.5)
    stable_output = (base_rates * device_spread * roughness).reshape(TOKEN_TOTAL, HEAD_TOTAL * HEAD_SIZE)
    spike_places = jax.random.randint(sequence_lanes[4], (2,), 0, TOKEN_TOTAL)
    spike_error = jax.random.uniform(sequence_lanes[5], (2, HEAD_TOTAL * HEAD_SIZE), jnp.float32, 0.22, 0.51)
    token_positions = jnp.arange(TOKEN_TOTAL)
    first_match = (token_positions == spike_places[0]).astype(jnp.float32)[:, None]
    second_match = (token_positions == spike_places[1]).astype(jnp.float32)[:, None]
    spike_events = first_match * spike_error[0][None, :] + second_match * spike_error[1][None, :]
    return -(stable_output + spike_events)


def draw_write_rate(key, part):
    slow_heads = head_kinds(key)
    sequence_lanes = jax.random.split(jax.random.fold_in(key, 13), 2)
    small_rates = jax.random.uniform(sequence_lanes[0], (TOKEN_TOTAL, HEAD_TOTAL), jnp.float32, 0.5, 2.5) * (HEAD_SIZE / (2.0 * TOKEN_TOTAL))
    large_rates = jax.random.uniform(sequence_lanes[1], (TOKEN_TOTAL, HEAD_TOTAL), jnp.float32, 0.2, 0.9)
    return jnp.where(slow_heads[None, :], small_rates, large_rates)


def block_levels(rng, dims, shards, smallest, largest):
    def one(position, parts):
        heights = jax.random.uniform(jax.random.fold_in(jax.random.fold_in(rng, 6), position), (parts,), jnp.float32, smallest / len(shards), largest / len(shards))
        return jnp.repeat(jnp.exp(heights), dims[position] // parts).reshape((-1,) + (1,) * (len(dims) - position - 1))

    factor_of = one(*shards[0])
    for cut in shards[1:]:
        factor_of = factor_of * one(*cut)
    return factor_of


def centred(stream_key, dims, width, most, pieces=(), held_as=jnp.bfloat16):
    loudness = block_levels(stream_key, dims, pieces, -0.22, 0.18) if pieces else 1.0
    values = jax.random.normal(stream_key, dims, jnp.float32) * width * loudness
    return jnp.minimum(jnp.maximum(values, -most), most).astype(held_as)


def setup_inputs(seed: int = 0) -> dict:
    seeds = jax.random.split(jax.random.key(seed), 9)
    query_vectors = centred(seeds[0], (TOKEN_TOTAL, HDK), 1.0, 6.0, ((0, 8), (1, 4)))
    key_vectors = draw_key_vectors(jax.random.fold_in(seeds[8], 71), 0)
    value_vectors = centred(seeds[2], (TOKEN_TOTAL, HDK), 1.0, 6.0, ((0, 8), (1, 4)))
    log_decay = draw_log_decay(jax.random.fold_in(seeds[8], 71), 0)
    write_rate = draw_write_rate(jax.random.fold_in(seeds[8], 71), 0)
    out_gate = centred(seeds[5], (TOKEN_TOTAL, HDK), 1.0, 6.0, ((0, 8), (1, 4)))
    norm_gain = jnp.clip(1.0 + 0.15 * jax.random.normal(seeds[6], (HEAD_SIZE,), jnp.float32), 0.25, 1.75)
    out_weight = centred(seeds[7], (HDK, D), HDK ** -0.5, 0.09375, ((0, 4),))
    return {"query_vectors": query_vectors, "key_vectors": key_vectors, "value_vectors": value_vectors, "log_decay": log_decay, "write_rate": write_rate, "out_gate": out_gate, "norm_gain": norm_gain, "out_weight": out_weight}


peak_value = lax.Precision.HIGHEST

def reference(query_vectors, key_vectors, value_vectors, log_decay, write_rate, out_gate, norm_gain, out_weight):
    queries = query_vectors.astype(jnp.float32).reshape(TOKEN_TOTAL, HEAD_TOTAL, HEAD_SIZE)
    raw_keys = key_vectors.astype(jnp.float32).reshape(TOKEN_TOTAL, HEAD_TOTAL, HEAD_SIZE)
    unit_keys = raw_keys / jnp.sqrt(lax.optimization_barrier(jnp.sum(raw_keys * raw_keys, axis=-1, keepdims=True)) + 1e-06)
    values = value_vectors.astype(jnp.float32).reshape(TOKEN_TOTAL, HEAD_TOTAL, HEAD_SIZE)
    decay_rates = jnp.exp(log_decay).reshape(TOKEN_TOTAL, HEAD_TOTAL, HEAD_SIZE)

    def token_step(state_matrix, inputs):
        query_vector_row, key_vector_row, value_row, factor, rate_now = inputs
        faded_state = state_matrix * factor[:, :, None]
        retrieved_value = jnp.einsum('rfl,rf->rl', faded_state, key_vector_row, precision=peak_value)
        update = rate_now[:, None] * (value_row - retrieved_value)
        state_matrix = faded_state + key_vector_row[:, :, None] * update[:, None, :]
        return (state_matrix, jnp.einsum('rfl,rf->rl', state_matrix, query_vector_row, precision=peak_value))
    initial = jnp.zeros((HEAD_TOTAL, HEAD_SIZE, HEAD_SIZE), jnp.float32)
    _, attended = lax.scan(token_step, initial, (queries, unit_keys, values, decay_rates, write_rate))
    mean_square = lax.optimization_barrier(jnp.mean(attended * attended, axis=-1, keepdims=True))
    gate_values = jax.nn.sigmoid(out_gate.astype(jnp.float32).reshape(TOKEN_TOTAL, HEAD_TOTAL, HEAD_SIZE))
    gated_out = attended / jnp.sqrt(mean_square + 1e-05) * norm_gain * gate_values
    gated_out = gated_out.astype(jnp.bfloat16).reshape(TOKEN_TOTAL, HEAD_TOTAL * HEAD_SIZE)
    group_width = HEAD_TOTAL // N_HEAD * HEAD_SIZE
    summed = jnp.zeros((TOKEN_TOTAL, D), jnp.float32)
    for group_index in range(N_HEAD):
        lower_col = group_index * group_width
        partial_value = jnp.dot(gated_out[:, lower_col:lower_col + group_width], out_weight[lower_col:lower_col + group_width], preferred_element_type=jnp.float32)
        summed = summed + lax.optimization_barrier(partial_value.astype(jnp.bfloat16)).astype(jnp.float32)
    return summed.astype(jnp.bfloat16)
```

```python
import functools

import jax
import jax.numpy as jnp
from jax import lax
from jax.experimental import pallas as pl
from jax.experimental.pallas import tpu as pltpu
from jax.sharding import PartitionSpec as P

HEAD_SIZE = 128
CHUNK = 128
PAIR = 2
F32 = jnp.float32
BF16 = jnp.bfloat16
NT = (((1,), (1,)), ((), ()))
TN = (((0,), (0,)), ((), ()))
NN = (((1,), (0,)), ((), ()))


def mm(left, right, dims=NN):
    return lax.dot_general(
        left.astype(BF16), right.astype(BF16), dims, preferred_element_type=F32
    )


def positions():
    later = lax.broadcasted_iota(jnp.int32, (CHUNK, CHUNK), 0)
    earlier = lax.broadcasted_iota(jnp.int32, (CHUNK, CHUNK), 1)
    return later, earlier


def maps_kernel(
    query_ref, key_ref, value_ref, decay_ref, rate_ref,
    map_ref, solved_ref, back_ref, now_ref, mid_ref, start_ref,
):
    chunk_count = key_ref.shape[0] // CHUNK
    first_head = pl.program_id(0) * PAIR
    later, earlier = positions()
    lower = (later >= earlier).astype(BF16)
    strict = later > earlier
    eye = (later == earlier).astype(F32)
    rates = rate_ref[...]
    rate_lane = lax.broadcasted_iota(jnp.int32, rates.shape, 1)
    units = [(i, j) for i in range(PAIR) for j in range(chunk_count)]
    rate_cols = [
        jnp.sum(jnp.where(rate_lane == first_head + i, rates, 0.0), axis=1, keepdims=True)
        for i in range(PAIR)
    ]

    def part(ref, unit):
        i, j = unit
        return ref[j * CHUNK : (j + 1) * CHUNK, i * HEAD_SIZE : (i + 1) * HEAD_SIZE]

    right, key_end, final, coupling, inverse = [], [], [], [], []
    for unit in units:
        i, j = unit
        rows = slice(j * CHUNK, (j + 1) * CHUNK)
        lanes = slice(i * HEAD_SIZE, (i + 1) * HEAD_SIZE)
        logs = part(decay_ref, unit)
        high = logs.astype(BF16)
        low = (logs - high.astype(F32)).astype(BF16)
        total = mm(lower, high) + mm(lower, low)
        middle = total[CHUNK // 2 - 1 : CHUNK // 2]
        last = total[CHUNK - 1 :]
        ahead = jnp.exp(total - middle)
        behind = jnp.exp(middle - total)
        mid_scale = jnp.exp(middle)
        keys = part(key_ref, unit).astype(F32)
        keys = keys * lax.rsqrt(jnp.sum(keys * keys, axis=1, keepdims=True) + 1e-06)
        rate = rate_cols[i][rows]
        key_now = keys * ahead
        key_back = keys * behind
        back_ref[rows, lanes] = key_back.astype(BF16)
        now_ref[rows, lanes] = (part(query_ref, unit).astype(F32) * ahead).astype(BF16)
        mid_ref[j : j + 1, lanes] = mid_scale
        coupling.append(jnp.where(strict, rate * mm(key_now, key_back, NT), 0.0))
        right.append(
            jnp.concatenate(
                [
                    (rate * key_now * mid_scale).astype(BF16),
                    (rate * part(value_ref, unit).astype(F32)).astype(BF16),
                ],
                axis=1,
            )
        )
        key_end.append((key_back * jnp.exp(last - middle)).astype(BF16))
        final.append(eye * jnp.exp(last))
    pair_mask = (later // 2) == (earlier // 2)
    inverse = [eye - jnp.where(pair_mask, c, 0.0) for c in coupling]
    width = 2
    while width < CHUNK:
        mask = ((later // (2 * width)) == (earlier // (2 * width))) & (
            (later // width) != (earlier // width)
        )
        inverse_low = [x.astype(BF16) for x in inverse]
        cross = [
            mm(x, jnp.where(mask, c, 0.0)).astype(BF16) for x, c in zip(inverse_low, coupling)
        ]
        inverse = [x - mm(y, z) for x, y, z in zip(inverse, cross, inverse_low)]
        width *= 2
    solved = [mm(x, r).astype(BF16) for x, r in zip(inverse, right)]
    carried = [mm(e, s, TN) for e, s in zip(key_end, solved)]
    for i in range(PAIR):
        running = None
        for j in range(chunk_count):
            u = i * chunk_count + j
            rows = slice(j * CHUNK, (j + 1) * CHUNK)
            solved_ref[rows, 2 * i * HEAD_SIZE : 2 * (i + 1) * HEAD_SIZE] = solved[u]
            step = final[u] - carried[u][:, :HEAD_SIZE]
            write = carried[u][:, HEAD_SIZE:]
            if running is None:
                running = jnp.concatenate([step, write], axis=1)
            else:
                held = running.astype(BF16)
                start_ref[i, j - 1] = held
                moved = mm(step, held)
                running = jnp.concatenate(
                    [moved[:, :HEAD_SIZE], moved[:, HEAD_SIZE:] + write], axis=1
                )
        map_ref[i] = running.astype(BF16)


def read_kernel(now_ref, back_ref, solved_ref, mid_ref, start_ref, through_ref, settled_ref):
    chunk_count = now_ref.shape[0] // CHUNK
    later, earlier = positions()
    lower = later >= earlier
    for i in range(PAIR):
        lanes = slice(i * HEAD_SIZE, (i + 1) * HEAD_SIZE)
        for j in range(chunk_count):
            rows = slice(j * CHUNK, (j + 1) * CHUNK)
            query = now_ref[rows, lanes]
            reading = jnp.where(lower, mm(query, back_ref[rows, lanes], NT), 0.0)
            mixed = mm(reading, solved_ref[rows, 2 * i * HEAD_SIZE : 2 * (i + 1) * HEAD_SIZE])
            effective = query.astype(F32) * mid_ref[j : j + 1, lanes] - mixed[:, :HEAD_SIZE]
            local = mixed[:, HEAD_SIZE:]
            if j:
                moved = mm(effective, start_ref[i, j - 1])
                through_ref[rows, lanes] = moved[:, :HEAD_SIZE].astype(BF16)
                settled_ref[rows, lanes] = moved[:, HEAD_SIZE:] + local
            else:
                through_ref[rows, lanes] = effective.astype(BF16)
                settled_ref[rows, lanes] = local


def chain_kernel(map_ref, state_ref):
    count = map_ref.shape[0]
    state = map_ref[0, :, HEAD_SIZE:].astype(F32)
    state_ref[0] = jnp.zeros((HEAD_SIZE, HEAD_SIZE), BF16)
    for turn in range(1, count):
        high = state.astype(BF16)
        state_ref[turn] = high
        if turn + 1 < count:
            low = (state - high.astype(F32)).astype(BF16)
            moved = mm(map_ref[turn, :, :HEAD_SIZE], jnp.concatenate([high, low], axis=1))
            state = (
                moved[:, :HEAD_SIZE]
                + moved[:, HEAD_SIZE:]
                + map_ref[turn, :, HEAD_SIZE:].astype(F32)
            )


def output_kernel(
    through_ref, settled_ref, gate_ref, state_ref, gain_ref, weight_ref, out_ref, gated_ref
):
    @pl.when(pl.program_id(0) == 0)
    def _():
        gain = gain_ref[...]
        for h in range(state_ref.shape[0]):
            lanes = slice(h * HEAD_SIZE, (h + 1) * HEAD_SIZE)
            attended = settled_ref[:, lanes] + mm(through_ref[:, lanes], state_ref[h])
            scale = lax.rsqrt(jnp.mean(attended * attended, axis=1, keepdims=True) + 1e-05)
            gate = jax.nn.sigmoid(gate_ref[:, lanes].astype(F32))
            gated_ref[:, lanes] = (attended * scale * gain * gate).astype(BF16)

    out_ref[...] = jnp.dot(
        gated_ref[...], weight_ref[...], preferred_element_type=F32
    ).astype(out_ref.dtype)


def entering(maps, axis):
    count = lax.axis_size(axis)
    head_count = maps.shape[0]
    if head_count == count:
        received = lax.all_to_all(maps, axis, 0, 0)
        states = pl.pallas_call(
            chain_kernel,
            out_shape=jax.ShapeDtypeStruct((count, HEAD_SIZE, HEAD_SIZE), BF16),
            name="chain",
        )(received)
        return lax.all_to_all(states, axis, 0, 0)
    gathered = lax.all_gather(maps, axis)

    def one(turn, state):
        item = lax.dynamic_index_in_dim(gathered, turn, 0, False)
        return (
            jnp.einsum(
                "hij,hjk->hik",
                item[..., :HEAD_SIZE].astype(F32),
                state,
                precision=lax.Precision.HIGHEST,
            )
            + item[..., HEAD_SIZE:]
        )

    zero = jnp.zeros((head_count, HEAD_SIZE, HEAD_SIZE), F32)
    return lax.fori_loop(0, lax.axis_index(axis), one, zero).astype(BF16)


def sum_heads(shares, axis):
    count = lax.axis_size(axis)
    if count % 2:
        return lax.psum_scatter(shares, axis, scatter_dimension=0, tiled=True)
    place = lax.axis_index(axis)
    core, chip = lax.rem(place, 2), lax.div(place, 2)
    chips = count // 2
    blocks = shares.reshape(chips, 2, shares.shape[0] // count, shares.shape[1])
    mine = lax.dynamic_index_in_dim(blocks, core, 1, False)
    other = lax.dynamic_index_in_dim(blocks, 1 - core, 1, False)
    came = lax.ppermute(other, axis, [(d, d ^ 1) for d in range(count)])
    both = mine.astype(F32) + came.astype(F32)
    total = lax.dynamic_index_in_dim(both, chip, 0, False)
    for turn in range(1, chips):
        target = lax.rem(chip + turn, chips)
        away = lax.dynamic_index_in_dim(both, target, 0, False).astype(BF16)
        hops = [(d, (d + 2 * turn) % count) for d in range(count)]
        total = total + lax.ppermute(away, axis, hops).astype(F32)
    return total.astype(BF16)


def on_device(
    query_vectors,
    key_vectors,
    value_vectors,
    log_decay,
    write_rate,
    out_gate,
    norm_gain,
    out_weight,
):
    rows, width = query_vectors.shape
    heads = width // HEAD_SIZE
    chunks = rows // CHUNK
    model = out_weight.shape[1]
    lanes = PAIR * HEAD_SIZE
    column = pl.BlockSpec((rows, lanes), lambda h: (0, h))
    double = pl.BlockSpec((rows, 2 * lanes), lambda h: (0, h))
    mid = pl.BlockSpec((chunks, lanes), lambda h: (0, h))
    start = pl.BlockSpec(
        (PAIR, chunks - 1, HEAD_SIZE, 2 * HEAD_SIZE), lambda h: (h, 0, 0, 0)
    )
    maps, solved, back, now, mids, starts = pl.pallas_call(
        maps_kernel,
        grid=(heads // PAIR,),
        in_specs=[
            column, column, column, column,
            pl.BlockSpec((rows, heads), lambda h: (0, 0)),
        ],
        out_specs=[
            pl.BlockSpec((PAIR, HEAD_SIZE, 2 * HEAD_SIZE), lambda h: (h, 0, 0)),
            double, column, column, mid, start,
        ],
        out_shape=[
            jax.ShapeDtypeStruct((heads, HEAD_SIZE, 2 * HEAD_SIZE), BF16),
            jax.ShapeDtypeStruct((rows, 2 * width), BF16),
            jax.ShapeDtypeStruct((rows, width), BF16),
            jax.ShapeDtypeStruct((rows, width), BF16),
            jax.ShapeDtypeStruct((chunks, width), F32),
            jax.ShapeDtypeStruct((heads, chunks - 1, HEAD_SIZE, 2 * HEAD_SIZE), BF16),
        ],
        compiler_params=pltpu.CompilerParams(vmem_limit_bytes=24 << 20),
        name="maps",
    )(query_vectors, key_vectors, value_vectors, log_decay, write_rate)
    through, settled = pl.pallas_call(
        read_kernel,
        grid=(heads // PAIR,),
        in_specs=[column, column, double, mid, start],
        out_specs=[column, column],
        out_shape=[
            jax.ShapeDtypeStruct((rows, width), BF16),
            jax.ShapeDtypeStruct((rows, width), F32),
        ],
        compiler_params=pltpu.CompilerParams(vmem_limit_bytes=16 << 20),
        name="read",
    )(now, back, solved, mids, starts)
    states = entering(maps, "ctx")
    tiles = 3 if model % (3 * 256) == 0 else 1
    whole = pl.BlockSpec((rows, width), lambda n: (0, 0))
    shares = pl.pallas_call(
        output_kernel,
        grid=(tiles,),
        in_specs=[
            whole, whole, whole,
            pl.BlockSpec((heads, HEAD_SIZE, HEAD_SIZE), lambda n: (0, 0, 0)),
            pl.BlockSpec((1, HEAD_SIZE), lambda n: (0, 0)),
            pl.BlockSpec((width, model // tiles), lambda n: (0, n)),
        ],
        out_specs=pl.BlockSpec((rows, model // tiles), lambda n: (0, n)),
        out_shape=jax.ShapeDtypeStruct((rows, model), BF16),
        scratch_shapes=[pltpu.VMEM((rows, width), BF16)],
        compiler_params=pltpu.CompilerParams(vmem_limit_bytes=32 << 20),
        name="output",
    )(through, settled, out_gate, states, norm_gain.reshape(1, HEAD_SIZE), out_weight)
    return sum_heads(shares, "head")


def solution(mesh):
    in_specs = (
        P("ctx", "head"),
        P("ctx", "head"),
        P("ctx", "head"),
        P("ctx", "head"),
        P("ctx", "head"),
        P("ctx", "head"),
        P(),
        P("head", None),
    )
    out_specs = P(("ctx", "head"), None)
    return jax.shard_map(
        on_device, mesh=mesh, in_specs=in_specs, out_specs=out_specs, check_vma=False
    )
```

```python
import functools

import jax
import jax.numpy as jnp
from jax import lax
from jax.experimental import pallas as pl
from jax.experimental.pallas import tpu as pltpu
from jax.sharding import PartitionSpec as P


HEAD_SIZE = 128
CHUNK = 128
PAIR = 2
LIMIT = 60
F32 = jnp.float32
BF16 = jnp.bfloat16
NT = (((1,), (1,)), ((), ()))
TN = (((0,), (0,)), ((), ()))
NN = (((1,), (0,)), ((), ()))


def mm(left, right, dims=NN):
    return lax.dot_general(
        left.astype(BF16), right.astype(BF16), dims, preferred_element_type=F32
    )


def positions():
    later = lax.broadcasted_iota(jnp.int32, (CHUNK, CHUNK), 0)
    earlier = lax.broadcasted_iota(jnp.int32, (CHUNK, CHUNK), 1)
    return later, earlier


def maps_kernel(
    top, slots, place_ref, query_ref, key_ref, value_ref, decay_ref, rate_ref, *refs
):
    slot_refs = refs[-(5 + slots) : -5]
    solved_ref, back_ref, now_ref, mid_ref, start_ref = refs[-5:]
    chunk_count = key_ref.shape[0] // CHUNK
    place = place_ref[0]
    first_head = ((place // PAIR) ^ (top - pl.program_id(0))) * PAIR
    later, earlier = positions()
    lower = (later >= earlier).astype(BF16)
    strict = later > earlier
    eye = (later == earlier).astype(F32)
    rates = rate_ref[...].T
    rate_lane = lax.broadcasted_iota(jnp.int32, rates.shape, 1)
    units = [(i, j) for i in range(PAIR) for j in range(chunk_count)]
    rate_cols = [
        jnp.sum(jnp.where(rate_lane == first_head + i, rates, 0.0), axis=1, keepdims=True)
        for i in range(PAIR)
    ]

    def part(ref, unit):
        i, j = unit
        return ref[j * CHUNK : (j + 1) * CHUNK, i * HEAD_SIZE : (i + 1) * HEAD_SIZE]

    right, key_end, final, coupling, inverse = [], [], [], [], []
    for unit in units:
        i, j = unit
        rows = slice(j * CHUNK, (j + 1) * CHUNK)
        lanes = slice(i * HEAD_SIZE, (i + 1) * HEAD_SIZE)
        logs = part(decay_ref, unit)
        high = logs.astype(BF16)
        low = (logs - high.astype(F32)).astype(BF16)
        total = mm(lower, high) + mm(lower, low)
        middle = total[CHUNK // 2 - 1 : CHUNK // 2]
        last = total[CHUNK - 1 :]
        ahead = jnp.exp(total - middle)
        behind = jnp.exp(middle - total)
        mid_scale = jnp.exp(middle)
        keys = part(key_ref, unit).astype(F32)
        keys = keys * lax.rsqrt(jnp.sum(keys * keys, axis=1, keepdims=True) + 1e-06)
        rate = rate_cols[i][rows]
        key_now = keys * ahead
        key_back = keys * behind
        back_ref[rows, lanes] = key_back.astype(BF16)
        now_ref[rows, lanes] = (part(query_ref, unit).astype(F32) * ahead).astype(BF16)
        mid_ref[j : j + 1, lanes] = mid_scale
        coupling.append(jnp.where(strict, rate * mm(key_now, key_back, NT), 0.0))
        right.append(
            jnp.concatenate(
                [
                    (rate * key_now * mid_scale).astype(BF16),
                    (rate * part(value_ref, unit).astype(F32)).astype(BF16),
                ],
                axis=1,
            )
        )
        key_end.append((key_back * jnp.exp(last - middle)).astype(BF16))
        final.append(eye * jnp.exp(last))
    pair_mask = (later // 2) == (earlier // 2)
    inverse = [eye - jnp.where(pair_mask, c, 0.0) for c in coupling]
    width = 2
    while width < CHUNK:
        mask = ((later // (2 * width)) == (earlier // (2 * width))) & (
            (later // width) != (earlier // width)
        )
        inverse_low = [x.astype(BF16) for x in inverse]
        cross = [
            mm(x, jnp.where(mask, c, 0.0)).astype(BF16) for x, c in zip(inverse_low, coupling)
        ]
        inverse = [x - mm(y, z) for x, y, z in zip(inverse, cross, inverse_low)]
        width *= 2
    solved = [mm(x, r).astype(BF16) for x, r in zip(inverse, right)]
    carried = [mm(e, s, TN) for e, s in zip(key_end, solved)]
    results = []
    for i in range(PAIR):
        running = None
        for j in range(chunk_count):
            u = i * chunk_count + j
            rows = slice(j * CHUNK, (j + 1) * CHUNK)
            solved_ref[rows, 2 * i * HEAD_SIZE : 2 * (i + 1) * HEAD_SIZE] = solved[u]
            step = final[u] - carried[u][:, :HEAD_SIZE]
            write = carried[u][:, HEAD_SIZE:]
            if running is None:
                running = jnp.concatenate([step, write], axis=1)
            else:
                held = running.astype(BF16)
                start_ref[i, j - 1] = held
                moved = mm(step, held)
                running = jnp.concatenate(
                    [moved[:, :HEAD_SIZE], moved[:, HEAD_SIZE:] + write], axis=1
                )
        results.append(running.astype(BF16))
    odd = (place & 1) == 1
    pair = [jnp.where(odd, results[1 - i], results[i]) for i in range(PAIR)]
    for s in range(slots // PAIR):

        @pl.when(pl.program_id(0) == s)
        def _():
            for i in range(PAIR):
                slot_refs[slots - PAIR * (s + 1) + i][...] = pair[i]


def read_kernel(now_ref, back_ref, solved_ref, mid_ref, start_ref, through_ref, settled_ref):
    chunk_count = now_ref.shape[0] // CHUNK
    later, earlier = positions()
    lower = later >= earlier
    for i in range(PAIR):
        lanes = slice(i * HEAD_SIZE, (i + 1) * HEAD_SIZE)
        for j in range(chunk_count):
            rows = slice(j * CHUNK, (j + 1) * CHUNK)
            query = now_ref[rows, lanes]
            reading = jnp.where(lower, mm(query, back_ref[rows, lanes], NT), 0.0)
            mixed = mm(reading, solved_ref[rows, 2 * i * HEAD_SIZE : 2 * (i + 1) * HEAD_SIZE])
            effective = query.astype(F32) * mid_ref[j : j + 1, lanes] - mixed[:, :HEAD_SIZE]
            local = mixed[:, HEAD_SIZE:]
            if j:
                moved = mm(effective, start_ref[i, j - 1])
                through_ref[rows, lanes] = moved[:, :HEAD_SIZE].astype(BF16)
                settled_ref[rows, lanes] = moved[:, HEAD_SIZE:] + local
            else:
                through_ref[rows, lanes] = effective.astype(BF16)
                settled_ref[rows, lanes] = local


def chain_kernel(place_ref, *refs):
    count = len(refs) - 2
    state_ref, map_ref = refs[count:]
    place = place_ref[0]
    for slot in range(count):
        map_ref[slot] = refs[slot][...]
    state = map_ref[place, :, HEAD_SIZE:].astype(F32)
    state_ref[0] = jnp.zeros((HEAD_SIZE, HEAD_SIZE), BF16)
    for turn in range(1, count):
        high = state.astype(BF16)
        state_ref[turn] = high
        if turn + 1 < count:
            slot = turn ^ place
            low = (state - high.astype(F32)).astype(BF16)
            moved = mm(map_ref[slot, :, :HEAD_SIZE], jnp.concatenate([high, low], axis=1))
            state = (
                moved[:, :HEAD_SIZE]
                + moved[:, HEAD_SIZE:]
                + map_ref[slot, :, HEAD_SIZE:].astype(F32)
            )


def output_kernel(
    place_ref, through_hbm, settled_hbm, gate_hbm, state_ref, gain_ref, weight_hbm,
    other_ref, mine_ref, through_ref, settled_ref, gate_ref, weight_ref, gated_ref, sems,
):
    core = place_ref[0]
    chips, block = other_ref.shape[:2]
    _, width = through_ref.shape
    heads = state_ref.shape[0]
    halves = 2
    span = width // halves
    tiles, tile = weight_ref.shape[0], weight_ref.shape[2]
    sources = [(through_hbm, through_ref), (settled_hbm, settled_ref), (gate_hbm, gate_ref)]
    copies, count = [], 0
    for half in range(halves):
        group = []
        for source, target in sources:
            for side in range(2):
                for chip in range(chips):
                    first = (2 * chip + (core if side else 1 - core)) * block
                    place = (side * chips + chip) * block
                    copy = pltpu.make_async_copy(
                        source.at[
                            pl.ds(pl.multiple_of(first, block), block),
                            pl.ds(half * span, span),
                        ],
                        target.at[pl.ds(place, block), pl.ds(half * span, span)],
                        sems.at[count],
                    )
                    copy.start()
                    group.append(copy)
                    count += 1
        copies.append(group)
    weights = []
    for n in range(tiles):
        copy = pltpu.make_async_copy(
            weight_hbm.at[:, pl.ds(n * tile, tile)], weight_ref.at[n], sems.at[count]
        )
        copy.start()
        weights.append(copy)
        count += 1
    gain = gain_ref[...]
    for half in range(halves):
        for copy in copies[half]:
            copy.wait()
        for h in range(half * heads // halves, (half + 1) * heads // halves):
            lanes = slice(h * HEAD_SIZE, (h + 1) * HEAD_SIZE)
            attended = settled_ref[:, lanes] + mm(through_ref[:, lanes], state_ref[h])
            scale = lax.rsqrt(jnp.mean(attended * attended, axis=1, keepdims=True) + 1e-05)
            gate = jax.nn.sigmoid(gate_ref[:, lanes].astype(F32))
            gated_ref[:, lanes] = (attended * scale * gain * gate).astype(BF16)
    for n in range(tiles):
        weights[n].wait()
        product = jnp.dot(gated_ref[...], weight_ref[n], preferred_element_type=F32)
        for side, target in enumerate((other_ref, mine_ref)):
            for chip in range(chips):
                place = (side * chips + chip) * block
                target[chip, :, n * tile : (n + 1) * tile] = product[
                    place : place + block
                ].astype(BF16)


def make_maps(operands, place, tops, previous):
    queries = operands[0]
    rows, width = queries.shape
    heads = operands[4].shape[0]
    chunks = rows // CHUNK
    lanes = PAIR * HEAD_SIZE
    top = max(tops)

    def pair(step, place_ref):
        return (place_ref[0] // PAIR) ^ (top - step)

    column = pl.BlockSpec((rows, lanes), lambda s, p: (0, pair(s, p)))
    slots = PAIR * len(tops)
    shapes = [jax.ShapeDtypeStruct((HEAD_SIZE, 2 * HEAD_SIZE), BF16)] * slots + [
        jax.ShapeDtypeStruct((rows, 2 * width), BF16),
        jax.ShapeDtypeStruct((rows, width), BF16),
        jax.ShapeDtypeStruct((rows, width), BF16),
        jax.ShapeDtypeStruct((chunks, width), F32),
        jax.ShapeDtypeStruct((heads, chunks - 1, HEAD_SIZE, 2 * HEAD_SIZE), BF16),
    ]
    share = len(tops) * PAIR * chunks
    return pl.pallas_call(
        functools.partial(maps_kernel, top, slots),
        grid_spec=pltpu.PrefetchScalarGridSpec(
            num_scalar_prefetch=1,
            grid=(len(tops),),
            in_specs=[column] * 4
            + [pl.BlockSpec((heads, rows), lambda s, p: (0, 0))]
            + [pl.BlockSpec(memory_space=pl.ANY)] * len(previous),
            out_specs=[pl.BlockSpec((HEAD_SIZE, 2 * HEAD_SIZE), lambda s, p: (0, 0))] * slots
            + [
                pl.BlockSpec((rows, 2 * lanes), lambda s, p: (0, pair(s, p))),
                column,
                column,
                pl.BlockSpec((chunks, lanes), lambda s, p: (0, pair(s, p))),
                pl.BlockSpec(
                    (PAIR, chunks - 1, HEAD_SIZE, 2 * HEAD_SIZE),
                    lambda s, p: (pair(s, p), 0, 0, 0),
                ),
            ],
        ),
        out_shape=shapes,
        input_output_aliases={6 + n: slots + n for n in range(len(previous))},
        cost_estimate=pl.CostEstimate(
            flops=share * 120_000_000, bytes_accessed=share * 400_000, transcendentals=0
        ),
        compiler_params=pltpu.CompilerParams(vmem_limit_bytes=LIMIT << 20),
        name="maps",
    )(place, *operands, *previous)


def finish_reading(held):
    solved, back, now, mids, starts = held
    rows, width = now.shape
    heads = width // HEAD_SIZE
    chunks = rows // CHUNK
    lanes = PAIR * HEAD_SIZE
    column = pl.BlockSpec((rows, lanes), lambda h: (0, h))
    return pl.pallas_call(
        read_kernel,
        grid=(heads // PAIR,),
        in_specs=[
            column,
            column,
            pl.BlockSpec((rows, 2 * lanes), lambda h: (0, h)),
            pl.BlockSpec((chunks, lanes), lambda h: (0, h)),
            pl.BlockSpec(
                (PAIR, chunks - 1, HEAD_SIZE, 2 * HEAD_SIZE), lambda h: (h, 0, 0, 0)
            ),
        ],
        out_specs=[column, column],
        out_shape=[
            jax.ShapeDtypeStruct((rows, width), BF16),
            jax.ShapeDtypeStruct((rows, width), F32),
        ],
        cost_estimate=pl.CostEstimate(
            flops=heads * chunks * 100_000_000,
            bytes_accessed=heads * chunks * 400_000,
            transcendentals=0,
        ),
        compiler_params=pltpu.CompilerParams(vmem_limit_bytes=LIMIT << 20),
        name="read",
    )(now, back, solved, mids, starts)


def project(core, through, settled, gates, states, gain, weight, groups):
    rows, width = through.shape
    heads = states.shape[0]
    model = weight.shape[1]
    chips = groups // 2
    block = rows // groups
    tiles = 3 if model % (3 * 256) == 0 else 1
    hbm = pl.BlockSpec(memory_space=pltpu.HBM)
    share = pl.BlockSpec((chips, block, model), lambda n, p: (0, 0, 0))
    return pl.pallas_call(
        output_kernel,
        grid_spec=pltpu.PrefetchScalarGridSpec(
            num_scalar_prefetch=1,
            grid=(1,),
            in_specs=[
                hbm,
                hbm,
                hbm,
                pl.BlockSpec((heads, HEAD_SIZE, HEAD_SIZE), lambda n, p: (0, 0, 0)),
                pl.BlockSpec((1, HEAD_SIZE), lambda n, p: (0, 0)),
                hbm,
            ],
            out_specs=[share, share],
            scratch_shapes=[
                pltpu.VMEM((rows, width), BF16),
                pltpu.VMEM((rows, width), F32),
                pltpu.VMEM((rows, width), BF16),
                pltpu.VMEM((tiles, width, model // tiles), BF16),
                pltpu.VMEM((rows, width), BF16),
                pltpu.SemaphoreType.DMA((12 * chips + tiles,)),
            ],
        ),
        out_shape=[jax.ShapeDtypeStruct((chips, block, model), BF16)] * 2,
        cost_estimate=pl.CostEstimate(
            flops=2 * rows * width * model,
            bytes_accessed=2 * width * model,
            transcendentals=0,
        ),
        compiler_params=pltpu.CompilerParams(vmem_limit_bytes=LIMIT << 20),
        name="output",
    )(
        jnp.reshape(core, (1,)).astype(jnp.int32),
        through,
        settled,
        gates,
        states,
        gain.reshape(1, HEAD_SIZE),
        weight,
    )


def carry_apart(operands, place, axis):
    count = lax.axis_size(axis)
    place_at = jnp.reshape(place, (1,)).astype(jnp.int32)

    def swap(block, turn):
        return lax.ppermute(block, axis, [(d, d ^ turn) for d in range(count)])

    pairs = count // PAIR
    half = pairs // 2
    received = [None] * count
    far = make_maps(operands, place_at, range(half, pairs), [])
    for r in range(PAIR * half, count):
        received[r] = swap(far[r - PAIR * half], r)
    near = make_maps(operands, place_at, range(half), far[-5:])
    received[0] = near[0]
    for r in range(1, PAIR * half):
        received[r] = swap(near[r], r)
    reads = finish_reading(near[-5:])
    block = pl.BlockSpec((HEAD_SIZE, 2 * HEAD_SIZE), lambda n, p: (0, 0))
    states = pl.pallas_call(
        chain_kernel,
        grid_spec=pltpu.PrefetchScalarGridSpec(
            num_scalar_prefetch=1,
            grid=(1,),
            in_specs=[block] * count,
            out_specs=pl.BlockSpec((count, HEAD_SIZE, HEAD_SIZE), lambda n, p: (0, 0, 0)),
            scratch_shapes=[pltpu.VMEM((count, HEAD_SIZE, 2 * HEAD_SIZE), BF16)],
        ),
        out_shape=jax.ShapeDtypeStruct((count, HEAD_SIZE, HEAD_SIZE), BF16),
        compiler_params=pltpu.CompilerParams(vmem_limit_bytes=8 << 20),
        name="chain",
    )(place_at, *received)
    return reads, lax.all_to_all(states, axis, 0, 0)


def carry_whole(operands, axis):
    heads = operands[4].shape[0]
    made = make_maps(operands, jnp.zeros((1,), jnp.int32), range(heads // PAIR), [])
    gathered = lax.all_gather(jnp.stack(made[:heads]), axis)

    def one(turn, state):
        item = lax.dynamic_index_in_dim(gathered, turn, 0, False).astype(F32)
        moved = jnp.einsum(
            "hij,hjk->hik", item[..., :HEAD_SIZE], state, precision=lax.Precision.HIGHEST
        )
        return moved + item[..., HEAD_SIZE:]

    zero = jnp.zeros((heads, HEAD_SIZE, HEAD_SIZE), F32)
    state = lax.fori_loop(0, lax.axis_index(axis), one, zero)
    return finish_reading(made[heads:]), state.astype(BF16)


def on_device(
    query_vectors,
    key_vectors,
    value_vectors,
    log_decay,
    write_rate,
    out_gate,
    norm_gain,
    out_weight,
):
    heads = query_vectors.shape[1] // HEAD_SIZE
    operands = [query_vectors, key_vectors, value_vectors, log_decay, write_rate.T]
    count = lax.axis_size("ctx")
    if heads == count and count & (count - 1) == 0 and count >= 4:
        reads, states = carry_apart(operands, lax.axis_index("ctx"), "ctx")
    else:
        reads, states = carry_whole(operands, "ctx")
    groups = lax.axis_size("head")
    place = lax.axis_index("head")
    core, chip = lax.rem(place, 2), lax.div(place, 2)
    chips = groups // 2

    other, mine = project(core, *reads, out_gate, states, norm_gain, out_weight, groups)
    came = lax.ppermute(other, "head", [(d, d ^ 1) for d in range(groups)])

    def both(block):
        return lax.dynamic_index_in_dim(mine, block, 0, False).astype(
            F32
        ) + lax.dynamic_index_in_dim(came, block, 0, False).astype(F32)

    total = both(chip)
    for turn in range(1, chips):
        away = both(lax.rem(chip + turn, chips)).astype(BF16)
        hops = [(d, (d + 2 * turn) % groups) for d in range(groups)]
        total = total + lax.ppermute(away, "head", hops).astype(F32)
    return total.astype(BF16)


def solution(mesh):
    in_specs = (
        P("ctx", "head"),
        P("ctx", "head"),
        P("ctx", "head"),
        P("ctx", "head"),
        P("ctx", "head"),
        P("ctx", "head"),
        P(),
        P("head", None),
    )
    out_specs = P(("ctx", "head"), None)

    return jax.shard_map(
        on_device, mesh=mesh, in_specs=in_specs, out_specs=out_specs, check_vma=False
    )
```

```python
import functools

import jax
import jax.numpy as jnp
from jax import lax
from jax.experimental import pallas as pl
from jax.experimental.pallas import tpu as pltpu
from jax.sharding import PartitionSpec as P


HEAD_SIZE = 128
CHUNK = 128
PAIR = 2
LIMIT = 24
F32 = jnp.float32
BF16 = jnp.bfloat16
NT = (((1,), (1,)), ((), ()))
TN = (((0,), (0,)), ((), ()))
NN = (((1,), (0,)), ((), ()))


def mm(left, right, dims=NN):
    return lax.dot_general(
        left.astype(BF16), right.astype(BF16), dims, preferred_element_type=F32
    )


def positions():
    later = lax.broadcasted_iota(jnp.int32, (CHUNK, CHUNK), 0)
    earlier = lax.broadcasted_iota(jnp.int32, (CHUNK, CHUNK), 1)
    return later, earlier


def maps_kernel(
    first_ref, query_ref, key_ref, value_ref, decay_ref, rate_ref, *refs
):
    map_ref, solved_ref, back_ref, now_ref, mid_ref, start_ref = refs[-6:]
    chunk_count = key_ref.shape[0] // CHUNK
    first_head = (first_ref[0] + pl.program_id(0)) * PAIR
    later, earlier = positions()
    lower = (later >= earlier).astype(BF16)
    strict = later > earlier
    eye = (later == earlier).astype(F32)
    rates = rate_ref[...].T
    rate_lane = lax.broadcasted_iota(jnp.int32, rates.shape, 1)
    units = [(i, j) for i in range(PAIR) for j in range(chunk_count)]
    rate_cols = [
        jnp.sum(jnp.where(rate_lane == first_head + i, rates, 0.0), axis=1, keepdims=True)
        for i in range(PAIR)
    ]

    def part(ref, unit):
        i, j = unit
        return ref[j * CHUNK : (j + 1) * CHUNK, i * HEAD_SIZE : (i + 1) * HEAD_SIZE]

    right, key_end, final, coupling, inverse = [], [], [], [], []
    for unit in units:
        i, j = unit
        rows = slice(j * CHUNK, (j + 1) * CHUNK)
        lanes = slice(i * HEAD_SIZE, (i + 1) * HEAD_SIZE)
        logs = part(decay_ref, unit)
        high = logs.astype(BF16)
        low = (logs - high.astype(F32)).astype(BF16)
        total = mm(lower, high) + mm(lower, low)
        middle = total[CHUNK // 2 - 1 : CHUNK // 2]
        last = total[CHUNK - 1 :]
        ahead = jnp.exp(total - middle)
        behind = jnp.exp(middle - total)
        mid_scale = jnp.exp(middle)
        keys = part(key_ref, unit).astype(F32)
        keys = keys * lax.rsqrt(jnp.sum(keys * keys, axis=1, keepdims=True) + 1e-06)
        rate = rate_cols[i][rows]
        key_now = keys * ahead
        key_back = keys * behind
        back_ref[rows, lanes] = key_back.astype(BF16)
        now_ref[rows, lanes] = (part(query_ref, unit).astype(F32) * ahead).astype(BF16)
        mid_ref[j : j + 1, lanes] = mid_scale
        coupling.append(jnp.where(strict, rate * mm(key_now, key_back, NT), 0.0))
        right.append(
            jnp.concatenate(
                [
                    (rate * key_now * mid_scale).astype(BF16),
                    (rate * part(value_ref, unit).astype(F32)).astype(BF16),
                ],
                axis=1,
            )
        )
        key_end.append((key_back * jnp.exp(last - middle)).astype(BF16))
        final.append(eye * jnp.exp(last))
    pair_mask = (later // 2) == (earlier // 2)
    inverse = [eye - jnp.where(pair_mask, c, 0.0) for c in coupling]
    width = 2
    while width < CHUNK:
        mask = ((later // (2 * width)) == (earlier // (2 * width))) & (
            (later // width) != (earlier // width)
        )
        inverse_low = [x.astype(BF16) for x in inverse]
        cross = [
            mm(x, jnp.where(mask, c, 0.0)).astype(BF16) for x, c in zip(inverse_low, coupling)
        ]
        inverse = [x - mm(y, z) for x, y, z in zip(inverse, cross, inverse_low)]
        width *= 2
    solved = [mm(x, r).astype(BF16) for x, r in zip(inverse, right)]
    carried = [mm(e, s, TN) for e, s in zip(key_end, solved)]
    for i in range(PAIR):
        running = None
        for j in range(chunk_count):
            u = i * chunk_count + j
            rows = slice(j * CHUNK, (j + 1) * CHUNK)
            solved_ref[rows, 2 * i * HEAD_SIZE : 2 * (i + 1) * HEAD_SIZE] = solved[u]
            step = final[u] - carried[u][:, :HEAD_SIZE]
            write = carried[u][:, HEAD_SIZE:]
            if running is None:
                running = jnp.concatenate([step, write], axis=1)
            else:
                held = running.astype(BF16)
                start_ref[i, j - 1] = held
                moved = mm(step, held)
                running = jnp.concatenate(
                    [moved[:, :HEAD_SIZE], moved[:, HEAD_SIZE:] + write], axis=1
                )
        map_ref[i] = running.astype(BF16)


def read_kernel(now_ref, back_ref, solved_ref, mid_ref, start_ref, through_ref, settled_ref):
    chunk_count = now_ref.shape[0] // CHUNK
    later, earlier = positions()
    lower = later >= earlier
    for i in range(PAIR):
        lanes = slice(i * HEAD_SIZE, (i + 1) * HEAD_SIZE)
        for j in range(chunk_count):
            rows = slice(j * CHUNK, (j + 1) * CHUNK)
            query = now_ref[rows, lanes]
            reading = jnp.where(lower, mm(query, back_ref[rows, lanes], NT), 0.0)
            mixed = mm(reading, solved_ref[rows, 2 * i * HEAD_SIZE : 2 * (i + 1) * HEAD_SIZE])
            effective = query.astype(F32) * mid_ref[j : j + 1, lanes] - mixed[:, :HEAD_SIZE]
            local = mixed[:, HEAD_SIZE:]
            if j:
                moved = mm(effective, start_ref[i, j - 1])
                through_ref[rows, lanes] = moved[:, :HEAD_SIZE].astype(BF16)
                settled_ref[rows, lanes] = moved[:, HEAD_SIZE:] + local
            else:
                through_ref[rows, lanes] = effective.astype(BF16)
                settled_ref[rows, lanes] = local


def follow(later, earlier):
    moved = mm(later[:, :HEAD_SIZE], earlier)
    width = earlier.shape[1]
    if width == HEAD_SIZE:
        return moved + later[:, HEAD_SIZE:].astype(F32)
    return jnp.concatenate(
        [
            moved[:, :HEAD_SIZE],
            moved[:, HEAD_SIZE:] + later[:, HEAD_SIZE:].astype(F32),
        ],
        axis=1,
    )


def join_kernel(place_ref, own_ref, came_ref, early_ref, *refs):
    slots, joined_ref = refs[:-1], refs[-1]
    second = place_ref[0] == 1
    for j in range(own_ref.shape[0]):
        own, came = own_ref[j], came_ref[j]
        early = jnp.where(second, came, own)
        early_ref[j] = early
        joined_ref[j] = follow(jnp.where(second, own, came), early).astype(BF16)
    for r in range(len(slots)):
        slots[r][...] = joined_ref[place_ref[1] ^ r]


def chain_kernel(place_ref, *refs):
    count = (len(refs) - 2) // 2
    came, slots = refs[:count], refs[count : 2 * count]
    map_ref, state_ref = refs[2 * count :]
    place = place_ref[1]
    for r in range(count):
        map_ref[r] = came[r][...]
    state_ref[0] = jnp.zeros((HEAD_SIZE, HEAD_SIZE), BF16)
    state = map_ref[place, :, HEAD_SIZE:].astype(F32)
    for turn in range(1, count):
        high = state.astype(BF16)
        state_ref[turn] = high
        if turn + 1 < count:
            item = map_ref[turn ^ place]
            low = (state - high.astype(F32)).astype(BF16)
            moved = mm(item[:, :HEAD_SIZE], jnp.concatenate([high, low], axis=1))
            state = (
                moved[:, :HEAD_SIZE] + moved[:, HEAD_SIZE:] + item[:, HEAD_SIZE:].astype(F32)
            )
    for r in range(count):
        slots[r][...] = state_ref[place ^ r]


def pass_kernel(place_ref, early_ref, *refs):
    count = len(refs) - 3
    keep_ref, send_ref, state_ref = refs[count:]
    second = place_ref[0] == 1
    for r in range(count):
        state_ref[place_ref[1] ^ r] = refs[r][...]
    for j in range(count):
        state = state_ref[j]
        after = follow(early_ref[j], state).astype(BF16)
        keep_ref[j] = jnp.where(second, after, state)
        send_ref[j] = jnp.where(second, state, after)


def output_kernel(
    split, place_ref, through_hbm, settled_hbm, gate_hbm, *refs
):
    parts, refs = refs[:split], refs[split:]
    gain_ref, weight_hbm, other_ref, mine_ref, through_ref = refs[:5]
    settled_ref, gate_ref, weight_ref, gated_ref, state_ref, sems = refs[5:]
    core = place_ref[0]
    each = parts[0].shape[0]
    for n, part in enumerate(parts):
        state_ref[pl.ds((place_ref[1] ^ n) * each, each)] = part[...]
    chips, block = other_ref.shape[:2]
    _, width = through_ref.shape
    heads = state_ref.shape[0]
    halves = 2
    span = width // halves
    tiles, tile = weight_ref.shape[0], weight_ref.shape[2]
    sources = [(through_hbm, through_ref), (settled_hbm, settled_ref), (gate_hbm, gate_ref)]
    copies, count = [], 0
    for half in range(halves):
        group = []
        for source, target in sources:
            for side in range(2):
                for chip in range(chips):
                    first = (2 * chip + (core if side else 1 - core)) * block
                    place = (side * chips + chip) * block
                    copy = pltpu.make_async_copy(
                        source.at[
                            pl.ds(pl.multiple_of(first, block), block),
                            pl.ds(half * span, span),
                        ],
                        target.at[pl.ds(place, block), pl.ds(half * span, span)],
                        sems.at[count],
                    )
                    copy.start()
                    group.append(copy)
                    count += 1
        copies.append(group)
    weights = []
    for n in range(tiles):
        copy = pltpu.make_async_copy(
            weight_hbm.at[:, pl.ds(n * tile, tile)], weight_ref.at[n], sems.at[count]
        )
        copy.start()
        weights.append(copy)
        count += 1
    gain = gain_ref[...]
    for half in range(halves):
        for copy in copies[half]:
            copy.wait()
        for h in range(half * heads // halves, (half + 1) * heads // halves):
            lanes = slice(h * HEAD_SIZE, (h + 1) * HEAD_SIZE)
            attended = settled_ref[:, lanes] + mm(through_ref[:, lanes], state_ref[h])
            scale = lax.rsqrt(jnp.mean(attended * attended, axis=1, keepdims=True) + 1e-05)
            gate = jax.nn.sigmoid(gate_ref[:, lanes].astype(F32))
            gated_ref[:, lanes] = (attended * scale * gain * gate).astype(BF16)
    for n in range(tiles):
        weights[n].wait()
        product = jnp.dot(gated_ref[...], weight_ref[n], preferred_element_type=F32)
        for side, target in enumerate((other_ref, mine_ref)):
            for chip in range(chips):
                place = (side * chips + chip) * block
                target[chip, :, n * tile : (n + 1) * tile] = product[
                    place : place + block
                ].astype(BF16)


def in_hbm(*arrays):
    return [pltpu.with_memory_space_constraint(a, pltpu.HBM) for a in arrays]


def make_maps(operands, first, pairs, previous):
    rows, width = operands[0].shape
    heads = operands[4].shape[0]
    chunks = rows // CHUNK
    lanes = PAIR * HEAD_SIZE
    column = pl.BlockSpec((rows, lanes), lambda s, p: (0, p[0] + s))
    share = pairs * PAIR * chunks
    return pl.pallas_call(
        maps_kernel,
        grid_spec=pltpu.PrefetchScalarGridSpec(
            num_scalar_prefetch=1,
            grid=(pairs,),
            in_specs=[column] * 4
            + [pl.BlockSpec((heads, rows), lambda s, p: (0, 0))]
            + [pl.BlockSpec(memory_space=pl.ANY)] * len(previous),
            out_specs=[
                pl.BlockSpec((PAIR, HEAD_SIZE, 2 * HEAD_SIZE), lambda s, p: (s, 0, 0)),
                pl.BlockSpec((rows, 2 * lanes), lambda s, p: (0, p[0] + s)),
                column,
                column,
                pl.BlockSpec((chunks, lanes), lambda s, p: (0, p[0] + s)),
                pl.BlockSpec(
                    (PAIR, chunks - 1, HEAD_SIZE, 2 * HEAD_SIZE),
                    lambda s, p: (p[0] + s, 0, 0, 0),
                ),
            ],
        ),
        out_shape=[
            jax.ShapeDtypeStruct((PAIR * pairs, HEAD_SIZE, 2 * HEAD_SIZE), BF16),
            pltpu.HBM((rows, 2 * width), BF16),
            pltpu.HBM((rows, width), BF16),
            pltpu.HBM((rows, width), BF16),
            pltpu.HBM((chunks, width), F32),
            pltpu.HBM((heads, chunks - 1, HEAD_SIZE, 2 * HEAD_SIZE), BF16),
        ],
        input_output_aliases={6 + n: 1 + n for n in range(len(previous))},
        cost_estimate=pl.CostEstimate(
            flops=share * 120_000_000, bytes_accessed=share * 400_000, transcendentals=0
        ),
        compiler_params=pltpu.CompilerParams(vmem_limit_bytes=LIMIT << 20),
    )(first, *operands, *previous)


def finish_reading(held):
    solved, back, now, mids, starts = held
    rows, width = now.shape
    heads = width // HEAD_SIZE
    chunks = rows // CHUNK
    lanes = PAIR * HEAD_SIZE
    column = pl.BlockSpec((rows, lanes), lambda h: (0, h))
    return pl.pallas_call(
        read_kernel,
        grid=(heads // PAIR,),
        in_specs=[
            column,
            column,
            pl.BlockSpec((rows, 2 * lanes), lambda h: (0, h)),
            pl.BlockSpec((chunks, lanes), lambda h: (0, h)),
            pl.BlockSpec(
                (PAIR, chunks - 1, HEAD_SIZE, 2 * HEAD_SIZE), lambda h: (h, 0, 0, 0)
            ),
        ],
        out_specs=[column, column],
        out_shape=[
            pltpu.HBM((rows, width), BF16),
            pltpu.HBM((rows, width), F32),
        ],
        cost_estimate=pl.CostEstimate(
            flops=heads * chunks * 100_000_000,
            bytes_accessed=heads * chunks * 400_000,
            transcendentals=0,
        ),
        compiler_params=pltpu.CompilerParams(vmem_limit_bytes=LIMIT << 20),
        name="read",
    )(*in_hbm(now, back, solved, mids, starts))


def project(places, through, settled, gates, states, gain, weight, groups):
    rows, width = through.shape
    heads = sum(part.shape[0] for part in states)
    model = weight.shape[1]
    chips = groups // 2
    block = rows // groups
    tiles = 3 if model % (3 * 256) == 0 else 1
    hbm = pl.BlockSpec(memory_space=pltpu.HBM)
    share = pl.BlockSpec((chips, block, model), lambda n, p: (0, 0, 0))
    return pl.pallas_call(
        functools.partial(output_kernel, len(states)),
        grid_spec=pltpu.PrefetchScalarGridSpec(
            num_scalar_prefetch=1,
            grid=(1,),
            in_specs=[
                hbm,
                hbm,
                hbm,
            ]
            + [pl.BlockSpec(part.shape, lambda n, p: (0, 0, 0)) for part in states]
            + [
                pl.BlockSpec((1, HEAD_SIZE), lambda n, p: (0, 0)),
                hbm,
            ],
            out_specs=[share, share],
            scratch_shapes=[
                pltpu.VMEM((rows, width), BF16),
                pltpu.VMEM((rows, width), F32),
                pltpu.VMEM((rows, width), BF16),
                pltpu.VMEM((tiles, width, model // tiles), BF16),
                pltpu.VMEM((rows, width), BF16),
                pltpu.VMEM((heads, HEAD_SIZE, HEAD_SIZE), BF16),
                pltpu.SemaphoreType.DMA((12 * chips + tiles,)),
            ],
        ),
        out_shape=[jax.ShapeDtypeStruct((chips, block, model), BF16)] * 2,
        cost_estimate=pl.CostEstimate(
            flops=2 * rows * width * model,
            bytes_accessed=2 * width * model,
            transcendentals=0,
        ),
        compiler_params=pltpu.CompilerParams(vmem_limit_bytes=LIMIT << 20),
        name="output",
    )(
        places,
        *in_hbm(through, settled, gates),
        *states,
        gain.reshape(1, HEAD_SIZE),
        *in_hbm(weight),
    )


def small_call(kernel, place, operands, shapes, scratch):
    def block(shape):
        return pl.BlockSpec(shape, lambda n, p: (0,) * len(shape))

    return pl.pallas_call(
        kernel,
        grid_spec=pltpu.PrefetchScalarGridSpec(
            num_scalar_prefetch=1,
            grid=(1,),
            in_specs=[block(a.shape) for a in operands],
            out_specs=[block(shape) for shape in shapes],
            scratch_shapes=[pltpu.VMEM(shape, BF16) for shape in scratch],
        ),
        out_shape=[jax.ShapeDtypeStruct(shape, BF16) for shape in shapes],
        compiler_params=pltpu.CompilerParams(vmem_limit_bytes=8 << 20),
    )(place, *operands)


def carry_apart(operands, place, axis):
    count = lax.axis_size(axis)
    half = count // 2
    side, turn = lax.rem(place, 2), lax.div(place, 2)
    place_at = jnp.stack([side, turn]).astype(jnp.int32)
    pairs = half // PAIR

    def swap(block, step):
        return lax.ppermute(block, axis, [(d, d ^ step) for d in range(count)])

    def first(group):
        return jnp.reshape(group * pairs, (1,)).astype(jnp.int32)

    item, square = (HEAD_SIZE, 2 * HEAD_SIZE), (HEAD_SIZE, HEAD_SIZE)
    far = make_maps(operands, first(1 - side), pairs, [])
    came = swap(far[0], 1)
    near = make_maps(operands, first(side), pairs, far[1:])
    early, *slots = small_call(
        join_kernel, place_at, [near[0], came], [(half, *item)] + [item] * half, [(half, *item)]
    )
    slots = [slots[0]] + [swap(slots[r], 2 * r) for r in range(1, half)]
    reads = finish_reading(near[1:])
    states = small_call(
        chain_kernel, place_at, slots, [square] * half, [(half, *item), (half, *square)]
    )
    states = [states[0]] + [swap(states[r], 2 * r) for r in range(1, half)]
    keep, send = small_call(
        pass_kernel, place_at, [early, *states], [(half, *square)] * 2, [(half, *square)]
    )
    return reads, [keep, swap(send, 1)], side


def carry_whole(operands, axis):
    heads = operands[4].shape[0]
    made = make_maps(operands, jnp.zeros((1,), jnp.int32), heads // PAIR, [])
    gathered = lax.all_gather(made[0], axis)

    def one(turn, state):
        item = lax.dynamic_index_in_dim(gathered, turn, 0, False).astype(F32)
        moved = jnp.einsum(
            "hij,hjk->hik", item[..., :HEAD_SIZE], state, precision=lax.Precision.HIGHEST
        )
        return moved + item[..., HEAD_SIZE:]

    zero = jnp.zeros((heads, HEAD_SIZE, HEAD_SIZE), F32)
    state = lax.fori_loop(0, lax.axis_index(axis), one, zero)
    return finish_reading(made[1:]), [state.astype(BF16)], 0


def on_device(
    query_vectors,
    key_vectors,
    value_vectors,
    log_decay,
    write_rate,
    out_gate,
    norm_gain,
    out_weight,
):
    heads = query_vectors.shape[1] // HEAD_SIZE
    operands = in_hbm(query_vectors, key_vectors, value_vectors, log_decay, write_rate.T)
    count = lax.axis_size("ctx")
    if heads == count and count & (count - 1) == 0 and count >= 8:
        reads, states, twist = carry_apart(operands, lax.axis_index("ctx"), "ctx")
    else:
        reads, states, twist = carry_whole(operands, "ctx")
    groups = lax.axis_size("head")
    place = lax.axis_index("head")
    core, chip = lax.rem(place, 2), lax.div(place, 2)
    chips = groups // 2

    places = jnp.stack([core, jnp.asarray(twist, core.dtype)]).astype(jnp.int32)
    other, mine = project(places, *reads, out_gate, states, norm_gain, out_weight, groups)
    came = lax.ppermute(other, "head", [(d, d ^ 1) for d in range(groups)])

    def both(block):
        return lax.dynamic_index_in_dim(mine, block, 0, False).astype(
            F32
        ) + lax.dynamic_index_in_dim(came, block, 0, False).astype(F32)

    total = both(chip)
    for turn in range(1, chips):
        away = both(lax.rem(chip + turn, chips)).astype(BF16)
        hops = [(d, (d + 2 * turn) % groups) for d in range(groups)]
        total = total + lax.ppermute(away, "head", hops).astype(F32)
    return total.astype(BF16)


def solution(mesh):
    in_specs = (
        P("ctx", "head"),
        P("ctx", "head"),
        P("ctx", "head"),
        P("ctx", "head"),
        P("ctx", "head"),
        P("ctx", "head"),
        P(),
        P("head", None),
    )
    out_specs = P(("ctx", "head"), None)

    return jax.shard_map(
        on_device, mesh=mesh, in_specs=in_specs, out_specs=out_specs, check_vma=False
    )
```

```python
import functools

import jax
import jax.numpy as jnp
from jax import lax
from jax.experimental import pallas as pl
from jax.experimental.pallas import tpu as pltpu
from jax.sharding import PartitionSpec as P


HEAD_SIZE = 128
CHUNK = 128
PAIR = 2
BATCH = 4
LIMIT = 24
PIECES = (2, 1)
F32 = jnp.float32
BF16 = jnp.bfloat16
NT = (((1,), (1,)), ((), ()))
TN = (((0,), (0,)), ((), ()))
NN = (((1,), (0,)), ((), ()))


def mm(left, right, dims=NN):
    return lax.dot_general(
        left.astype(BF16), right.astype(BF16), dims, preferred_element_type=F32
    )


def positions():
    later = lax.broadcasted_iota(jnp.int32, (CHUNK, CHUNK), 0)
    earlier = lax.broadcasted_iota(jnp.int32, (CHUNK, CHUNK), 1)
    return later, earlier


def maps_kernel(
    first_ref, query_ref, key_ref, value_ref, decay_ref, rate_ref, *refs
):
    map_ref, solved_ref, back_ref, now_ref, mid_ref, start_ref = refs[-6:]
    chunk_count = key_ref.shape[0] // CHUNK
    first_head = (first_ref[0] + pl.program_id(0)) * BATCH
    later, earlier = positions()
    lower = (later >= earlier).astype(BF16)
    strict = later > earlier
    eye = (later == earlier).astype(F32)
    rates = rate_ref[...].T
    rate_lane = lax.broadcasted_iota(jnp.int32, rates.shape, 1)
    units = [(i, j) for i in range(BATCH) for j in range(chunk_count)]
    rate_cols = [
        jnp.sum(jnp.where(rate_lane == first_head + i, rates, 0.0), axis=1, keepdims=True)
        for i in range(BATCH)
    ]

    def part(ref, unit):
        i, j = unit
        return ref[j * CHUNK : (j + 1) * CHUNK, i * HEAD_SIZE : (i + 1) * HEAD_SIZE]

    right, key_end, final, coupling, inverse = [], [], [], [], []
    for unit in units:
        i, j = unit
        rows = slice(j * CHUNK, (j + 1) * CHUNK)
        lanes = slice(i * HEAD_SIZE, (i + 1) * HEAD_SIZE)
        logs = part(decay_ref, unit)
        high = logs.astype(BF16)
        low = (logs - high.astype(F32)).astype(BF16)
        total = mm(lower, high) + mm(lower, low)
        middle = total[CHUNK // 2 - 1 : CHUNK // 2]
        last = total[CHUNK - 1 :]
        ahead = jnp.exp(total - middle)
        behind = jnp.exp(middle - total)
        mid_scale = jnp.exp(middle)
        keys = part(key_ref, unit).astype(F32)
        keys = keys * lax.rsqrt(jnp.sum(keys * keys, axis=1, keepdims=True) + 1e-06)
        rate = rate_cols[i][rows]
        key_now = keys * ahead
        key_back = keys * behind
        back_ref[rows, lanes] = key_back.astype(BF16)
        now_ref[rows, lanes] = (part(query_ref, unit).astype(F32) * ahead).astype(BF16)
        mid_ref[j : j + 1, lanes] = mid_scale
        coupling.append(jnp.where(strict, rate * mm(key_now, key_back, NT), 0.0))
        right.append(
            jnp.concatenate(
                [
                    (rate * key_now * mid_scale).astype(BF16),
                    (rate * part(value_ref, unit).astype(F32)).astype(BF16),
                ],
                axis=1,
            )
        )
        key_end.append((key_back * jnp.exp(last - middle)).astype(BF16))
        final.append(eye * jnp.exp(last))
    pair_mask = (later // 2) == (earlier // 2)
    inverse = [eye - jnp.where(pair_mask, c, 0.0) for c in coupling]
    width = 2
    while width < CHUNK:
        mask = ((later // (2 * width)) == (earlier // (2 * width))) & (
            (later // width) != (earlier // width)
        )
        inverse_low = [x.astype(BF16) for x in inverse]
        cross = [
            mm(x, jnp.where(mask, c, 0.0)).astype(BF16) for x, c in zip(inverse_low, coupling)
        ]
        inverse = [x - mm(y, z) for x, y, z in zip(inverse, cross, inverse_low)]
        width *= 2
    solved = [mm(x, r).astype(BF16) for x, r in zip(inverse, right)]
    carried = [mm(e, s, TN) for e, s in zip(key_end, solved)]
    for i in range(BATCH):
        running = None
        for j in range(chunk_count):
            u = i * chunk_count + j
            rows = slice(j * CHUNK, (j + 1) * CHUNK)
            solved_ref[rows, 2 * i * HEAD_SIZE : 2 * (i + 1) * HEAD_SIZE] = solved[u]
            step = final[u] - carried[u][:, :HEAD_SIZE]
            write = carried[u][:, HEAD_SIZE:]
            if running is None:
                running = jnp.concatenate([step, write], axis=1)
            else:
                held = running.astype(BF16)
                start_ref[i, j - 1] = held
                moved = mm(step, held)
                running = jnp.concatenate(
                    [moved[:, :HEAD_SIZE], moved[:, HEAD_SIZE:] + write], axis=1
                )
        map_ref[i] = running.astype(BF16)


def read_kernel(now_ref, back_ref, solved_ref, mid_ref, start_ref, *refs):
    through_ref, settled_ref = refs[-2:]
    chunk_count = now_ref.shape[0] // CHUNK
    later, earlier = positions()
    lower = later >= earlier
    for i in range(PAIR):
        lanes = slice(i * HEAD_SIZE, (i + 1) * HEAD_SIZE)
        for j in range(chunk_count):
            rows = slice(j * CHUNK, (j + 1) * CHUNK)
            query = now_ref[rows, lanes]
            reading = jnp.where(lower, mm(query, back_ref[rows, lanes], NT), 0.0)
            mixed = mm(reading, solved_ref[rows, 2 * i * HEAD_SIZE : 2 * (i + 1) * HEAD_SIZE])
            effective = query.astype(F32) * mid_ref[j : j + 1, lanes] - mixed[:, :HEAD_SIZE]
            local = mixed[:, HEAD_SIZE:]
            if j:
                moved = mm(effective, start_ref[i, j - 1])
                through_ref[rows, lanes] = moved[:, :HEAD_SIZE].astype(BF16)
                settled_ref[rows, lanes] = moved[:, HEAD_SIZE:] + local
            else:
                through_ref[rows, lanes] = effective.astype(BF16)
                settled_ref[rows, lanes] = local


def follow(maps, states):
    moved = mm(maps[:, :HEAD_SIZE], states)
    written = maps[:, HEAD_SIZE:].astype(F32)
    if states.shape[1] == HEAD_SIZE:
        return moved + written
    return jnp.concatenate([moved[:, :HEAD_SIZE], moved[:, HEAD_SIZE:] + written], axis=1)


def join_kernel(level, place_ref, own_ref, came_ref, early_ref, keep_ref, send_ref, joined_ref):
    second = place_ref[level] == 1
    half = keep_ref.shape[0]
    for j in range(own_ref.shape[0]):
        own, came = own_ref[j], came_ref[j]
        early = jnp.where(second, came, own)
        early_ref[j] = early
        joined_ref[j] = follow(jnp.where(second, own, came), early).astype(BF16)
    for j in range(half):
        keep_ref[j] = joined_ref[place_ref[level + 1] * half + j]
        send_ref[j] = joined_ref[(1 - place_ref[level + 1]) * half + j]


def crest_kernel(level, place_ref, own_ref, came_ref, early_ref, send_ref):
    second = place_ref[level] == 1
    for j in range(own_ref.shape[0]):
        own, came = own_ref[j], came_ref[j]
        early = jnp.where(second, came, own)
        early_ref[j] = early
        late = jnp.where(second, own, came)
        send_ref[j] = follow(late, early[:, HEAD_SIZE:]).astype(BF16)


def turn_kernel(level, place_ref, early_ref, came_ref, keep_ref, send_ref):
    second, later = place_ref[level] == 1, place_ref[level + 1] == 1
    for j in range(early_ref.shape[0]):
        came = came_ref[j]
        state = jnp.where(later, came, jnp.zeros_like(came))
        after = follow(early_ref[j], state).astype(BF16)
        keep_ref[j] = jnp.where(second, after, state)
        send_ref[j] = jnp.where(second, state, after)


def pass_kernel(level, place_ref, early_ref, own_ref, came_ref, keep_ref, send_ref, state_ref):
    second = place_ref[level] == 1
    half = own_ref.shape[0]
    for j in range(half):
        state_ref[place_ref[level + 1] * half + j] = own_ref[j]
        state_ref[(1 - place_ref[level + 1]) * half + j] = came_ref[j]
    for j in range(2 * half):
        state = state_ref[j]
        after = follow(early_ref[j], state).astype(BF16)
        keep_ref[j] = jnp.where(second, after, state)
        send_ref[j] = jnp.where(second, state, after)


def output_kernel(
    split, place_ref, through_hbm, settled_hbm, gate_hbm, *refs
):
    parts, refs = refs[:split], refs[split:]
    gain_ref, weight_hbm, other_ref, mine_ref, through_ref = refs[:5]
    settled_ref, gate_ref, weight_ref, gated_ref, state_ref, sems = refs[5:]
    core = place_ref[0]
    each = parts[0].shape[0]
    for n, part in enumerate(parts):
        state_ref[pl.ds((place_ref[1] ^ n) * each, each)] = part[...]
    chips, block = other_ref.shape[:2]
    _, width = through_ref.shape
    heads = state_ref.shape[0]
    halves = 2
    span = width // halves
    tiles, tile = weight_ref.shape[0], weight_ref.shape[2]
    sources = [(through_hbm, through_ref), (settled_hbm, settled_ref), (gate_hbm, gate_ref)]
    copies, count = [], 0
    for half in range(halves):
        group = []
        for source, target in sources:
            for side in range(2):
                for chip in range(chips):
                    first = (2 * chip + (core if side else 1 - core)) * block
                    place = (side * chips + chip) * block
                    copy = pltpu.make_async_copy(
                        source.at[
                            pl.ds(pl.multiple_of(first, block), block),
                            pl.ds(half * span, span),
                        ],
                        target.at[pl.ds(place, block), pl.ds(half * span, span)],
                        sems.at[count],
                    )
                    copy.start()
                    group.append(copy)
                    count += 1
        copies.append(group)
    weights = []
    for n in range(tiles):
        copy = pltpu.make_async_copy(
            weight_hbm.at[:, pl.ds(n * tile, tile)], weight_ref.at[n], sems.at[count]
        )
        copy.start()
        weights.append(copy)
        count += 1
    gain = gain_ref[...]
    for half in range(halves):
        for copy in copies[half]:
            copy.wait()
        for h in range(half * heads // halves, (half + 1) * heads // halves):
            lanes = slice(h * HEAD_SIZE, (h + 1) * HEAD_SIZE)
            attended = settled_ref[:, lanes] + mm(through_ref[:, lanes], state_ref[h])
            scale = lax.rsqrt(jnp.mean(attended * attended, axis=1, keepdims=True) + 1e-05)
            gate = jax.nn.sigmoid(gate_ref[:, lanes].astype(F32))
            gated_ref[:, lanes] = (attended * scale * gain * gate).astype(BF16)
    for n in range(tiles):
        weights[n].wait()
        product = jnp.dot(gated_ref[...], weight_ref[n], preferred_element_type=F32)
        for side, target in enumerate((other_ref, mine_ref)):
            for chip in range(chips):
                place = (side * chips + chip) * block
                target[chip, :, n * tile : (n + 1) * tile] = product[
                    place : place + block
                ].astype(BF16)


def in_hbm(*arrays):
    return [pltpu.with_memory_space_constraint(a, pltpu.HBM) for a in arrays]


def make_maps(operands, first, pairs, previous):
    rows, width = operands[0].shape
    heads = operands[4].shape[0]
    chunks = rows // CHUNK
    lanes = BATCH * HEAD_SIZE
    column = pl.BlockSpec((rows, lanes), lambda s, p: (0, p[0] + s))
    share = pairs * BATCH * chunks
    return pl.pallas_call(
        maps_kernel,
        grid_spec=pltpu.PrefetchScalarGridSpec(
            num_scalar_prefetch=1,
            grid=(pairs,),
            in_specs=[column] * 4
            + [pl.BlockSpec((heads, rows), lambda s, p: (0, 0))]
            + [pl.BlockSpec(memory_space=pltpu.HBM)] * len(previous),
            out_specs=[
                pl.BlockSpec((BATCH, HEAD_SIZE, 2 * HEAD_SIZE), lambda s, p: (s, 0, 0)),
                pl.BlockSpec((rows, 2 * lanes), lambda s, p: (0, p[0] + s)),
                column,
                column,
                pl.BlockSpec((chunks, lanes), lambda s, p: (0, p[0] + s)),
                pl.BlockSpec(
                    (BATCH, chunks - 1, HEAD_SIZE, 2 * HEAD_SIZE),
                    lambda s, p: (p[0] + s, 0, 0, 0),
                ),
            ],
        ),
        out_shape=[
            jax.ShapeDtypeStruct((BATCH * pairs, HEAD_SIZE, 2 * HEAD_SIZE), BF16),
            pltpu.HBM((rows, 2 * width), BF16),
            pltpu.HBM((rows, width), BF16),
            pltpu.HBM((rows, width), BF16),
            pltpu.HBM((chunks, width), F32),
            pltpu.HBM((heads, chunks - 1, HEAD_SIZE, 2 * HEAD_SIZE), BF16),
        ],
        input_output_aliases={6 + n: 1 + n for n in range(len(previous))},
        cost_estimate=pl.CostEstimate(
            flops=share * 120_000_000, bytes_accessed=share * 400_000, transcendentals=0
        ),
        compiler_params=pltpu.CompilerParams(vmem_limit_bytes=LIMIT << 20),
    )(first, *operands, *previous)


def finish_reading(held, first, pairs, previous):
    solved, back, now, mids, starts = held
    rows, width = now.shape
    chunks = rows // CHUNK
    lanes = PAIR * HEAD_SIZE
    column = pl.BlockSpec((rows, lanes), lambda h: (0, first + h))
    return pl.pallas_call(
        read_kernel,
        grid=(pairs,),
        in_specs=[
            column,
            column,
            pl.BlockSpec((rows, 2 * lanes), lambda h: (0, first + h)),
            pl.BlockSpec((chunks, lanes), lambda h: (0, first + h)),
            pl.BlockSpec(
                (PAIR, chunks - 1, HEAD_SIZE, 2 * HEAD_SIZE), lambda h: (first + h, 0, 0, 0)
            ),
        ]
        + [pl.BlockSpec(memory_space=pltpu.HBM)] * len(previous),
        out_specs=[column, column],
        out_shape=[pltpu.HBM((rows, width), BF16), pltpu.HBM((rows, width), F32)],
        input_output_aliases={5 + n: n for n in range(len(previous))},
        cost_estimate=pl.CostEstimate(
            flops=pairs * PAIR * chunks * 100_000_000,
            bytes_accessed=pairs * PAIR * chunks * 400_000,
            transcendentals=0,
        ),
        compiler_params=pltpu.CompilerParams(vmem_limit_bytes=LIMIT << 20),
    )(*in_hbm(now, back, solved, mids, starts), *previous)


def project(places, through, settled, gates, states, gain, weight, groups):
    rows, width = through.shape
    heads = sum(part.shape[0] for part in states)
    model = weight.shape[1]
    chips = groups // 2
    block = rows // groups
    tiles = 3 if model % (3 * 256) == 0 else 1
    hbm = pl.BlockSpec(memory_space=pltpu.HBM)
    share = pl.BlockSpec((chips, block, model), lambda n, p: (0, 0, 0))
    return pl.pallas_call(
        functools.partial(output_kernel, len(states)),
        grid_spec=pltpu.PrefetchScalarGridSpec(
            num_scalar_prefetch=1,
            grid=(1,),
            in_specs=[
                hbm,
                hbm,
                hbm,
            ]
            + [pl.BlockSpec(part.shape, lambda n, p: (0, 0, 0)) for part in states]
            + [
                pl.BlockSpec((1, HEAD_SIZE), lambda n, p: (0, 0)),
                hbm,
            ],
            out_specs=[share, share],
            scratch_shapes=[
                pltpu.VMEM((rows, width), BF16),
                pltpu.VMEM((rows, width), F32),
                pltpu.VMEM((rows, width), BF16),
                pltpu.VMEM((tiles, width, model // tiles), BF16),
                pltpu.VMEM((rows, width), BF16),
                pltpu.VMEM((heads, HEAD_SIZE, HEAD_SIZE), BF16),
                pltpu.SemaphoreType.DMA((12 * chips + tiles,)),
            ],
        ),
        out_shape=[jax.ShapeDtypeStruct((chips, block, model), BF16)] * 2,
        cost_estimate=pl.CostEstimate(
            flops=2 * rows * width * model,
            bytes_accessed=2 * width * model,
            transcendentals=0,
        ),
        compiler_params=pltpu.CompilerParams(vmem_limit_bytes=LIMIT << 20),
        name="output",
    )(
        places,
        *in_hbm(through, settled, gates),
        *states,
        gain.reshape(1, HEAD_SIZE),
        *in_hbm(weight),
    )


def small_call(kernel, place, operands, shapes, scratch):
    def block(shape):
        return pl.BlockSpec(shape, lambda n, p: (0,) * len(shape))

    return pl.pallas_call(
        kernel,
        grid_spec=pltpu.PrefetchScalarGridSpec(
            num_scalar_prefetch=1,
            grid=(1,),
            in_specs=[block(a.shape) for a in operands],
            out_specs=[block(shape) for shape in shapes],
            scratch_shapes=[pltpu.VMEM(shape, BF16) for shape in scratch],
        ),
        out_shape=[jax.ShapeDtypeStruct(shape, BF16) for shape in shapes],
        compiler_params=pltpu.CompilerParams(vmem_limit_bytes=8 << 20),
    )(place, *operands)


def carry_apart(operands, place, axis):
    count = lax.axis_size(axis)
    heads = operands[4].shape[0]
    bits = [lax.rem(lax.div(place, 1 << n), 2) for n in range(3)]
    place_at = jnp.stack(bits).astype(jnp.int32)
    half, quarter = heads // 2, heads // 4
    pairs, batches = half // PAIR, half // BATCH

    def swap(block, step):
        return lax.ppermute(block, axis, [(d, d ^ step) for d in range(count)])

    def first(group):
        return jnp.reshape(group * batches, (1,)).astype(jnp.int32)

    item, square = (HEAD_SIZE, 2 * HEAD_SIZE), (HEAD_SIZE, HEAD_SIZE)
    far = make_maps(operands, first(1 - bits[0]), batches, [])
    came = swap(far[0], 1)
    near = make_maps(operands, first(bits[0]), batches, far[1:])
    held = near[1:]
    early, keep, send = small_call(
        functools.partial(join_kernel, 0),
        place_at,
        [near[0], came],
        [(half, *item), (quarter, *item), (quarter, *item)],
        [(half, *item)],
    )
    came = swap(send, 2)
    reads = finish_reading(held, 0, PIECES[0], [])
    crest, send = small_call(
        functools.partial(crest_kernel, 1),
        place_at,
        [keep, came],
        [(quarter, *item), (quarter, *square)],
        [],
    )
    came = swap(send, 4)
    reads = finish_reading(held, PIECES[0], PIECES[1], reads)
    keep, send = small_call(
        functools.partial(turn_kernel, 1), place_at, [crest, came], [(quarter, *square)] * 2, []
    )
    came = swap(send, 2)
    done = PIECES[0] + PIECES[1]
    reads = finish_reading(held, done, 2 * pairs - done, reads)
    keep, send = small_call(
        functools.partial(pass_kernel, 0),
        place_at,
        [early, keep, came],
        [(half, *square)] * 2,
        [(half, *square)],
    )
    return reads, [keep, swap(send, 1)], bits[0]


def carry_whole(operands, axis):
    heads = operands[4].shape[0]
    made = make_maps(operands, jnp.zeros((1,), jnp.int32), heads // BATCH, [])
    gathered = lax.all_gather(made[0], axis)

    def one(turn, state):
        item = lax.dynamic_index_in_dim(gathered, turn, 0, False).astype(F32)
        moved = jnp.einsum(
            "hij,hjk->hik", item[..., :HEAD_SIZE], state, precision=lax.Precision.HIGHEST
        )
        return moved + item[..., HEAD_SIZE:]

    zero = jnp.zeros((heads, HEAD_SIZE, HEAD_SIZE), F32)
    state = lax.fori_loop(0, lax.axis_index(axis), one, zero)
    reads = finish_reading(made[1:], 0, heads // PAIR, [])
    return reads, [state.astype(BF16)], 0


def on_device(
    query_vectors,
    key_vectors,
    value_vectors,
    log_decay,
    write_rate,
    out_gate,
    norm_gain,
    out_weight,
):
    heads = query_vectors.shape[1] // HEAD_SIZE
    operands = in_hbm(query_vectors, key_vectors, value_vectors, log_decay, write_rate.T)
    count = lax.axis_size("ctx")
    if count == 8 and heads == 8:
        reads, states, twist = carry_apart(operands, lax.axis_index("ctx"), "ctx")
    else:
        reads, states, twist = carry_whole(operands, "ctx")
    groups = lax.axis_size("head")
    place = lax.axis_index("head")
    core, chip = lax.rem(place, 2), lax.div(place, 2)
    chips = groups // 2

    places = jnp.stack([core, jnp.asarray(twist, core.dtype)]).astype(jnp.int32)
    other, mine = project(places, *reads, out_gate, states, norm_gain, out_weight, groups)
    came = lax.ppermute(other, "head", [(d, d ^ 1) for d in range(groups)])

    def both(block):
        return lax.dynamic_index_in_dim(mine, block, 0, False).astype(
            F32
        ) + lax.dynamic_index_in_dim(came, block, 0, False).astype(F32)

    total = both(chip)
    for turn in range(1, chips):
        away = both(lax.rem(chip + turn, chips)).astype(BF16)
        hops = [(d, (d + 2 * turn) % groups) for d in range(groups)]
        total = total + lax.ppermute(away, "head", hops).astype(F32)
    return total.astype(BF16)


def solution(mesh):
    in_specs = (
        P("ctx", "head"),
        P("ctx", "head"),
        P("ctx", "head"),
        P("ctx", "head"),
        P("ctx", "head"),
        P("ctx", "head"),
        P(),
        P("head", None),
    )
    out_specs = P(("ctx", "head"), None)

    return jax.shard_map(
        on_device, mesh=mesh, in_specs=in_specs, out_specs=out_specs, check_vma=False
    )
```

```python
import functools

import jax
import jax.numpy as jnp
from jax import lax
from jax.experimental import pallas as pl
from jax.experimental.pallas import tpu as pltpu
from jax.sharding import PartitionSpec as P


HEAD_SIZE = 128
CHUNK = 128
BATCH = 4
LIMIT = 24
F32 = jnp.float32
BF16 = jnp.bfloat16
NT = (((1,), (1,)), ((), ()))
TN = (((0,), (0,)), ((), ()))
NN = (((1,), (0,)), ((), ()))


def mm(left, right, dims=NN):
    return lax.dot_general(
        left.astype(BF16), right.astype(BF16), dims, preferred_element_type=F32
    )


def positions():
    later = lax.broadcasted_iota(jnp.int32, (CHUNK, CHUNK), 0)
    earlier = lax.broadcasted_iota(jnp.int32, (CHUNK, CHUNK), 1)
    return later, earlier


def maps_kernel(
    first_ref, query_ref, key_ref, value_ref, decay_ref, rate_ref, *refs
):
    map_ref, through_ref, settled_ref = refs[-3:]
    chunk_count = key_ref.shape[0] // CHUNK
    first_head = (first_ref[0] + pl.program_id(0)) * BATCH
    later, earlier = positions()
    ones = (later >= earlier).astype(BF16)
    strict = later > earlier
    eye = (later == earlier).astype(F32)
    rates = rate_ref[...].T
    rate_lane = lax.broadcasted_iota(jnp.int32, rates.shape, 1)
    units = [(i, j) for i in range(BATCH) for j in range(chunk_count)]
    rate_cols = [
        jnp.sum(jnp.where(rate_lane == first_head + i, rates, 0.0), axis=1, keepdims=True)
        for i in range(BATCH)
    ]

    def part(ref, unit):
        i, j = unit
        return ref[j * CHUNK : (j + 1) * CHUNK, i * HEAD_SIZE : (i + 1) * HEAD_SIZE]

    right, key_end, final, coupling, inverse = [], [], [], [], []
    now, back, mid = [], [], []
    for unit in units:
        i, j = unit
        rows = slice(j * CHUNK, (j + 1) * CHUNK)
        logs = part(decay_ref, unit)
        high = logs.astype(BF16)
        low = (logs - high.astype(F32)).astype(BF16)
        total = mm(ones, high) + mm(ones, low)
        middle = total[CHUNK // 2 - 1 : CHUNK // 2]
        last = total[CHUNK - 1 :]
        ahead = jnp.exp(total - middle)
        behind = jnp.exp(middle - total)
        mid_scale = jnp.exp(middle)
        keys = part(key_ref, unit).astype(F32)
        keys = keys * lax.rsqrt(jnp.sum(keys * keys, axis=1, keepdims=True) + 1e-06)
        rate = rate_cols[i][rows]
        key_now = keys * ahead
        key_back = keys * behind
        now.append((part(query_ref, unit).astype(F32) * ahead).astype(BF16))
        back.append(key_back.astype(BF16))
        mid.append(mid_scale)
        coupling.append(jnp.where(strict, rate * mm(key_now, key_back, NT), 0.0))
        right.append(
            jnp.concatenate(
                [
                    (rate * key_now * mid_scale).astype(BF16),
                    (rate * part(value_ref, unit).astype(F32)).astype(BF16),
                ],
                axis=1,
            )
        )
        key_end.append((key_back * jnp.exp(last - middle)).astype(BF16))
        final.append(eye * jnp.exp(last))
    pair_mask = (later // 2) == (earlier // 2)
    inverse = [eye - jnp.where(pair_mask, c, 0.0) for c in coupling]
    width = 2
    while width < CHUNK:
        mask = ((later // (2 * width)) == (earlier // (2 * width))) & (
            (later // width) != (earlier // width)
        )
        inverse_low = [x.astype(BF16) for x in inverse]
        cross = [
            mm(x, jnp.where(mask, c, 0.0)).astype(BF16) for x, c in zip(inverse_low, coupling)
        ]
        inverse = [x - mm(y, z) for x, y, z in zip(inverse, cross, inverse_low)]
        width *= 2
    solved = [mm(x, r).astype(BF16) for x, r in zip(inverse, right)]
    carried = [mm(e, s, TN) for e, s in zip(key_end, solved)]
    lower = later >= earlier
    reading = [jnp.where(lower, mm(q, k, NT), 0.0) for q, k in zip(now, back)]
    mixed = [mm(r, s) for r, s in zip(reading, solved)]
    for i in range(BATCH):
        lanes = slice(i * HEAD_SIZE, (i + 1) * HEAD_SIZE)
        running = None
        for j in range(chunk_count):
            u = i * chunk_count + j
            rows = slice(j * CHUNK, (j + 1) * CHUNK)
            effective = now[u].astype(F32) * mid[u] - mixed[u][:, :HEAD_SIZE]
            local = mixed[u][:, HEAD_SIZE:]
            step = final[u] - carried[u][:, :HEAD_SIZE]
            write = carried[u][:, HEAD_SIZE:]
            if running is None:
                through_ref[rows, lanes] = effective.astype(BF16)
                settled_ref[rows, lanes] = local
                running = jnp.concatenate([step, write], axis=1)
            else:
                held = running.astype(BF16)
                seen = mm(effective, held)
                through_ref[rows, lanes] = seen[:, :HEAD_SIZE].astype(BF16)
                settled_ref[rows, lanes] = seen[:, HEAD_SIZE:] + local
                moved = mm(step, held)
                running = jnp.concatenate(
                    [moved[:, :HEAD_SIZE], moved[:, HEAD_SIZE:] + write], axis=1
                )
        map_ref[i] = running.astype(BF16)


def follow(maps, states):
    moved = mm(maps[:, :HEAD_SIZE], states)
    written = maps[:, HEAD_SIZE:].astype(F32)
    if states.shape[1] == HEAD_SIZE:
        return moved + written
    return jnp.concatenate([moved[:, :HEAD_SIZE], moved[:, HEAD_SIZE:] + written], axis=1)


def join_kernel(level, place_ref, own_ref, came_ref, early_ref, keep_ref, send_ref, joined_ref):
    second = place_ref[level] == 1
    half = keep_ref.shape[0]
    for j in range(own_ref.shape[0]):
        own, came = own_ref[j], came_ref[j]
        early = jnp.where(second, came, own)
        early_ref[j] = early
        joined_ref[j] = follow(jnp.where(second, own, came), early).astype(BF16)
    for j in range(half):
        keep_ref[j] = joined_ref[place_ref[level + 1] * half + j]
        send_ref[j] = joined_ref[(1 - place_ref[level + 1]) * half + j]


def crest_kernel(level, place_ref, own_ref, came_ref, early_ref, send_ref):
    second = place_ref[level] == 1
    for j in range(own_ref.shape[0]):
        own, came = own_ref[j], came_ref[j]
        early = jnp.where(second, came, own)
        early_ref[j] = early
        late = jnp.where(second, own, came)
        send_ref[j] = follow(late, early[:, HEAD_SIZE:]).astype(BF16)


def turn_kernel(level, place_ref, early_ref, came_ref, keep_ref, send_ref):
    second, later = place_ref[level] == 1, place_ref[level + 1] == 1
    for j in range(early_ref.shape[0]):
        came = came_ref[j]
        state = jnp.where(later, came, jnp.zeros_like(came))
        after = follow(early_ref[j], state).astype(BF16)
        keep_ref[j] = jnp.where(second, after, state)
        send_ref[j] = jnp.where(second, state, after)


def pass_kernel(level, place_ref, early_ref, own_ref, came_ref, keep_ref, send_ref, state_ref):
    second = place_ref[level] == 1
    half = own_ref.shape[0]
    for j in range(half):
        state_ref[place_ref[level + 1] * half + j] = own_ref[j]
        state_ref[(1 - place_ref[level + 1]) * half + j] = came_ref[j]
    for j in range(2 * half):
        state = state_ref[j]
        after = follow(early_ref[j], state).astype(BF16)
        keep_ref[j] = jnp.where(second, after, state)
        send_ref[j] = jnp.where(second, state, after)


def gate_heads(through_ref, settled_ref, gate_ref, state_ref, gain_ref, gated_ref):
    gain = gain_ref[...]
    for h in range(state_ref.shape[0]):
        lanes = slice(h * HEAD_SIZE, (h + 1) * HEAD_SIZE)
        attended = settled_ref[:, lanes] + mm(through_ref[:, lanes], state_ref[h])
        scale = lax.rsqrt(jnp.mean(attended * attended, axis=1, keepdims=True) + 1e-05)
        gate = jax.nn.sigmoid(gate_ref[:, lanes].astype(F32))
        gated_ref[:, lanes] = (attended * scale * gain * gate).astype(BF16)


def tile_spans(model):
    tile = model // 3 if model % 768 == 0 else model
    return [slice(n, n + tile) for n in range(0, model, tile)]


def early_kernel(
    chips, place_ref, through_hbm, settled_hbm, gate_hbm, weight_hbm, state_ref, gain_ref,
    total_ref, through_rest, settled_rest, gate_rest, weight_rest,
    through_ref, settled_ref, gate_ref, weight_ref, gated_ref, sems,
):
    core, side = place_ref[0], place_ref[1]
    rows, span = through_ref.shape
    block = rows // (2 * chips)
    waits = []

    def load(source, target):
        copy = pltpu.make_async_copy(source, target, sems.at[len(waits)])
        copy.start()
        waits.append(copy)

    def load_group(group, targets, weight_target):
        columns = pl.ds(pl.multiple_of(group * span, span), span)
        for source, target in zip((through_hbm, settled_hbm, gate_hbm), targets):
            for own in range(2):
                for chip in range(chips):
                    first = (2 * chip + (core if own else 1 - core)) * block
                    load(
                        source.at[pl.ds(pl.multiple_of(first, block), block), columns],
                        target.at[pl.ds((own * chips + chip) * block, block)],
                    )
        load(weight_hbm.at[columns], weight_target)

    load_group(side, (through_ref, settled_ref, gate_ref), weight_ref)
    near = len(waits)
    load_group(1 - side, (through_rest, settled_rest, gate_rest), weight_rest)
    for copy in waits[: near - 1]:
        copy.wait()
    gate_heads(through_ref, settled_ref, gate_ref, state_ref, gain_ref, gated_ref)
    waits[near - 1].wait()
    for tile in tile_spans(weight_ref.shape[1]):
        total_ref[:, tile] = jnp.dot(
            gated_ref[...], weight_ref[:, tile], preferred_element_type=F32
        )
    for copy in waits[near:]:
        copy.wait()


def late_kernel(
    through_ref, settled_ref, gate_ref, weight_ref, total_ref, state_ref, gain_ref,
    other_ref, mine_ref, gated_ref,
):
    chips, block = other_ref.shape[:2]
    gate_heads(through_ref, settled_ref, gate_ref, state_ref, gain_ref, gated_ref)
    for tile in tile_spans(weight_ref.shape[1]):
        product = total_ref[:, tile] + jnp.dot(
            gated_ref[...], weight_ref[:, tile], preferred_element_type=F32
        )
        for own, target in enumerate((other_ref, mine_ref)):
            for chip in range(chips):
                first = (own * chips + chip) * block
                target[chip, :, tile] = product[first : first + block].astype(BF16)


def in_hbm(*arrays):
    return [pltpu.with_memory_space_constraint(a, pltpu.HBM) for a in arrays]


def make_maps(operands, first, pairs, previous):
    rows, width = operands[0].shape
    heads = operands[4].shape[0]
    chunks = rows // CHUNK
    lanes = BATCH * HEAD_SIZE
    column = pl.BlockSpec((rows, lanes), lambda s, p: (0, p[0] + s))
    share = pairs * BATCH * chunks
    return pl.pallas_call(
        maps_kernel,
        grid_spec=pltpu.PrefetchScalarGridSpec(
            num_scalar_prefetch=1,
            grid=(pairs,),
            in_specs=[column] * 4
            + [pl.BlockSpec((heads, rows), lambda s, p: (0, 0))]
            + [pl.BlockSpec(memory_space=pltpu.HBM)] * len(previous),
            out_specs=[
                pl.BlockSpec((BATCH, HEAD_SIZE, 2 * HEAD_SIZE), lambda s, p: (s, 0, 0)),
                column,
                column,
            ],
        ),
        out_shape=[
            jax.ShapeDtypeStruct((BATCH * pairs, HEAD_SIZE, 2 * HEAD_SIZE), BF16),
            pltpu.HBM((rows, width), BF16),
            pltpu.HBM((rows, width), F32),
        ],
        input_output_aliases={6 + n: 1 + n for n in range(len(previous))},
        cost_estimate=pl.CostEstimate(
            flops=share * 120_000_000, bytes_accessed=share * 400_000, transcendentals=0
        ),
        compiler_params=pltpu.CompilerParams(vmem_limit_bytes=LIMIT << 20),
    )(first, *operands, *previous)


def project(places, through, settled, gates, states, gain, weight, groups):
    rows, width = through.shape
    model = weight.shape[1]
    chips = groups // 2
    block = rows // groups
    span = width // 2
    vmem = pl.BlockSpec(memory_space=pltpu.VMEM)
    hbm = pl.BlockSpec(memory_space=pltpu.HBM)
    keep, came = states
    gain = gain.reshape(1, HEAD_SIZE)
    pieces = [((rows, span), BF16), ((rows, span), F32), ((rows, span), BF16)]
    pieces.append(((span, model), BF16))
    grant = pltpu.CompilerParams(vmem_limit_bytes=LIMIT << 20)
    cost = pl.CostEstimate(
        flops=rows * width * model, bytes_accessed=2 * width * model, transcendentals=0
    )
    total, *rest = pl.pallas_call(
        functools.partial(early_kernel, chips),
        in_specs=[pl.BlockSpec(memory_space=pltpu.SMEM)] + [hbm] * 4 + [vmem] * 2,
        out_specs=[vmem] * 5,
        out_shape=[pltpu.VMEM((rows, model), F32)] + [pltpu.VMEM(*p) for p in pieces],
        scratch_shapes=[pltpu.VMEM(*p) for p in pieces]
        + [
            pltpu.VMEM((rows, span), BF16),
            pltpu.SemaphoreType.DMA((12 * chips + 2,)),
        ],
        cost_estimate=cost,
        compiler_params=grant,
        name="early",
    )(places, *in_hbm(through, settled, gates, weight), keep, gain)
    return pl.pallas_call(
        late_kernel,
        in_specs=[vmem] * 7,
        out_specs=[vmem] * 2,
        out_shape=[jax.ShapeDtypeStruct((chips, block, model), BF16)] * 2,
        scratch_shapes=[pltpu.VMEM((rows, span), BF16)],
        cost_estimate=cost,
        compiler_params=grant,
        name="late",
    )(*rest, total, came, gain)


def small_call(kernel, place, operands, shapes, scratch):
    def block(shape):
        return pl.BlockSpec(shape, lambda n, p: (0,) * len(shape))

    return pl.pallas_call(
        kernel,
        grid_spec=pltpu.PrefetchScalarGridSpec(
            num_scalar_prefetch=1,
            grid=(1,),
            in_specs=[block(a.shape) for a in operands],
            out_specs=[block(shape) for shape in shapes],
            scratch_shapes=[pltpu.VMEM(shape, BF16) for shape in scratch],
        ),
        out_shape=[jax.ShapeDtypeStruct(shape, BF16) for shape in shapes],
        compiler_params=pltpu.CompilerParams(vmem_limit_bytes=8 << 20),
    )(place, *operands)


def carry_apart(operands, place, axis):
    count = lax.axis_size(axis)
    heads = operands[4].shape[0]
    bits = [lax.rem(lax.div(place, 1 << n), 2) for n in range(3)]
    place_at = jnp.stack(bits).astype(jnp.int32)
    half, quarter = heads // 2, heads // 4
    batches = half // BATCH

    def swap(block, step):
        return lax.ppermute(block, axis, [(d, d ^ step) for d in range(count)])

    def first(group):
        return jnp.reshape(group * batches, (1,)).astype(jnp.int32)

    item, square = (HEAD_SIZE, 2 * HEAD_SIZE), (HEAD_SIZE, HEAD_SIZE)
    far = make_maps(operands, first(1 - bits[0]), batches, [])
    came = swap(far[0], 1)
    near = make_maps(operands, first(bits[0]), batches, far[1:])
    early, keep, send = small_call(
        functools.partial(join_kernel, 0),
        place_at,
        [near[0], came],
        [(half, *item), (quarter, *item), (quarter, *item)],
        [(half, *item)],
    )
    came = swap(send, 2)
    crest, send = small_call(
        functools.partial(crest_kernel, 1),
        place_at,
        [keep, came],
        [(quarter, *item), (quarter, *square)],
        [],
    )
    came = swap(send, 4)
    keep, send = small_call(
        functools.partial(turn_kernel, 1), place_at, [crest, came], [(quarter, *square)] * 2, []
    )
    came = swap(send, 2)
    keep, send = small_call(
        functools.partial(pass_kernel, 0),
        place_at,
        [early, keep, came],
        [(half, *square)] * 2,
        [(half, *square)],
    )
    return near[1:], [keep, swap(send, 1)], bits[0]


def carry_whole(operands, axis):
    heads = operands[4].shape[0]
    made = make_maps(operands, jnp.zeros((1,), jnp.int32), heads // BATCH, [])
    gathered = lax.all_gather(made[0], axis)

    def one(turn, state):
        item = lax.dynamic_index_in_dim(gathered, turn, 0, False).astype(F32)
        moved = jnp.einsum(
            "hij,hjk->hik", item[..., :HEAD_SIZE], state, precision=lax.Precision.HIGHEST
        )
        return moved + item[..., HEAD_SIZE:]

    zero = jnp.zeros((heads, HEAD_SIZE, HEAD_SIZE), F32)
    state = lax.fori_loop(0, lax.axis_index(axis), one, zero)
    return made[1:], jnp.split(state.astype(BF16), 2), 0


def on_device(
    query_vectors,
    key_vectors,
    value_vectors,
    log_decay,
    write_rate,
    out_gate,
    norm_gain,
    out_weight,
):
    heads = query_vectors.shape[1] // HEAD_SIZE
    operands = in_hbm(query_vectors, key_vectors, value_vectors, log_decay, write_rate.T)
    count = lax.axis_size("ctx")
    if count == 8 and heads == 8:
        reads, states, twist = carry_apart(operands, lax.axis_index("ctx"), "ctx")
    else:
        reads, states, twist = carry_whole(operands, "ctx")
    groups = lax.axis_size("head")
    place = lax.axis_index("head")
    core, chip = lax.rem(place, 2), lax.div(place, 2)
    chips = groups // 2

    places = jnp.stack([core, jnp.asarray(twist, core.dtype)]).astype(jnp.int32)
    other, mine = project(places, *reads, out_gate, states, norm_gain, out_weight, groups)
    came = lax.ppermute(other, "head", [(d, d ^ 1) for d in range(groups)])

    def both(block):
        return lax.dynamic_index_in_dim(mine, block, 0, False).astype(
            F32
        ) + lax.dynamic_index_in_dim(came, block, 0, False).astype(F32)

    total = both(chip)
    for turn in range(1, chips):
        away = both(lax.rem(chip + turn, chips)).astype(BF16)
        hops = [(d, (d + 2 * turn) % groups) for d in range(groups)]
        total = total + lax.ppermute(away, "head", hops).astype(F32)
    return total.astype(BF16)


def solution(mesh):
    in_specs = (
        P("ctx", "head"),
        P("ctx", "head"),
        P("ctx", "head"),
        P("ctx", "head"),
        P("ctx", "head"),
        P("ctx", "head"),
        P(),
        P("head", None),
    )
    out_specs = P(("ctx", "head"), None)

    return jax.shard_map(
        on_device, mesh=mesh, in_specs=in_specs, out_specs=out_specs, check_vma=False
    )
```

```python
import functools

import jax
import jax.numpy as jnp
from jax import lax
from jax.experimental import pallas as pl
from jax.experimental.pallas import tpu as pltpu
from jax.sharding import PartitionSpec as P


HEAD_SIZE = 128
CHUNK = 128
BATCH = 4
LIMIT = 24
F32 = jnp.float32
BF16 = jnp.bfloat16
NT = (((1,), (1,)), ((), ()))
TN = (((0,), (0,)), ((), ()))
NN = (((1,), (0,)), ((), ()))


def mm(left, right, dims=NN):
    return lax.dot_general(
        left.astype(BF16), right.astype(BF16), dims, preferred_element_type=F32
    )


def positions():
    later = lax.broadcasted_iota(jnp.int32, (CHUNK, CHUNK), 0)
    earlier = lax.broadcasted_iota(jnp.int32, (CHUNK, CHUNK), 1)
    return later, earlier


def maps_kernel(
    first_ref, query_ref, key_ref, value_ref, decay_ref, rate_ref, *refs
):
    map_ref, through_ref, settled_ref = refs[-3:]
    chunk_count = key_ref.shape[0] // CHUNK
    first_head = (first_ref[0] + pl.program_id(0)) * BATCH
    later, earlier = positions()
    ones = (later >= earlier).astype(BF16)
    strict = later > earlier
    eye = (later == earlier).astype(F32)
    rates = rate_ref[...].T
    rate_lane = lax.broadcasted_iota(jnp.int32, rates.shape, 1)
    units = [(i, j) for i in range(BATCH) for j in range(chunk_count)]
    rate_cols = [
        jnp.sum(jnp.where(rate_lane == first_head + i, rates, 0.0), axis=1, keepdims=True)
        for i in range(BATCH)
    ]

    def part(ref, unit):
        i, j = unit
        return ref[j * CHUNK : (j + 1) * CHUNK, i * HEAD_SIZE : (i + 1) * HEAD_SIZE]

    right, key_end, final, coupling, inverse = [], [], [], [], []
    now, back, mid = [], [], []
    for unit in units:
        i, j = unit
        rows = slice(j * CHUNK, (j + 1) * CHUNK)
        logs = part(decay_ref, unit)
        high = logs.astype(BF16)
        low = (logs - high.astype(F32)).astype(BF16)
        total = mm(ones, high) + mm(ones, low)
        middle = total[CHUNK // 2 - 1 : CHUNK // 2]
        last = total[CHUNK - 1 :]
        ahead = jnp.exp(total - middle)
        behind = jnp.exp(middle - total)
        mid_scale = jnp.exp(middle)
        keys = part(key_ref, unit).astype(F32)
        keys = keys * lax.rsqrt(jnp.sum(keys * keys, axis=1, keepdims=True) + 1e-06)
        rate = rate_cols[i][rows]
        key_now = keys * ahead
        key_back = keys * behind
        now.append((part(query_ref, unit).astype(F32) * ahead).astype(BF16))
        back.append(key_back.astype(BF16))
        mid.append(mid_scale)
        coupling.append(jnp.where(strict, rate * mm(key_now, key_back, NT), 0.0))
        right.append(
            jnp.concatenate(
                [
                    (rate * key_now * mid_scale).astype(BF16),
                    (rate * part(value_ref, unit).astype(F32)).astype(BF16),
                ],
                axis=1,
            )
        )
        key_end.append((key_back * jnp.exp(last - middle)).astype(BF16))
        final.append(eye * jnp.exp(last))
    pair_mask = (later // 2) == (earlier // 2)
    inverse = [eye - jnp.where(pair_mask, c, 0.0) for c in coupling]
    width = 2
    while width < CHUNK:
        mask = ((later // (2 * width)) == (earlier // (2 * width))) & (
            (later // width) != (earlier // width)
        )
        inverse_low = [x.astype(BF16) for x in inverse]
        cross = [
            mm(x, jnp.where(mask, c, 0.0)).astype(BF16) for x, c in zip(inverse_low, coupling)
        ]
        inverse = [x - mm(y, z) for x, y, z in zip(inverse, cross, inverse_low)]
        width *= 2
    solved = [mm(x, r).astype(BF16) for x, r in zip(inverse, right)]
    carried = [mm(e, s, TN) for e, s in zip(key_end, solved)]
    lower = later >= earlier
    reading = [jnp.where(lower, mm(q, k, NT), 0.0) for q, k in zip(now, back)]
    mixed = [mm(r, s) for r, s in zip(reading, solved)]
    for i in range(BATCH):
        lanes = slice(i * HEAD_SIZE, (i + 1) * HEAD_SIZE)
        running = None
        for j in range(chunk_count):
            u = i * chunk_count + j
            rows = slice(j * CHUNK, (j + 1) * CHUNK)
            effective = now[u].astype(F32) * mid[u] - mixed[u][:, :HEAD_SIZE]
            local = mixed[u][:, HEAD_SIZE:]
            step = final[u] - carried[u][:, :HEAD_SIZE]
            write = carried[u][:, HEAD_SIZE:]
            if running is None:
                through_ref[rows, lanes] = effective.astype(BF16)
                settled_ref[rows, lanes] = local
                running = jnp.concatenate([step, write], axis=1)
            else:
                held = running.astype(BF16)
                seen = mm(effective, held)
                through_ref[rows, lanes] = seen[:, :HEAD_SIZE].astype(BF16)
                settled_ref[rows, lanes] = seen[:, HEAD_SIZE:] + local
                moved = mm(step, held)
                running = jnp.concatenate(
                    [moved[:, :HEAD_SIZE], moved[:, HEAD_SIZE:] + write], axis=1
                )
        map_ref[i] = running.astype(BF16)


def follow(maps, states):
    moved = mm(maps[:, :HEAD_SIZE], states)
    written = maps[:, HEAD_SIZE:].astype(F32)
    if states.shape[1] == HEAD_SIZE:
        return moved + written
    return jnp.concatenate([moved[:, :HEAD_SIZE], moved[:, HEAD_SIZE:] + written], axis=1)


def join_kernel(level, place_ref, own_ref, came_ref, early_ref, keep_ref, send_ref, joined_ref):
    second = place_ref[level] == 1
    half = keep_ref.shape[0]
    for j in range(own_ref.shape[0]):
        own, came = own_ref[j], came_ref[j]
        early = jnp.where(second, came, own)
        early_ref[j] = early
        joined_ref[j] = follow(jnp.where(second, own, came), early).astype(BF16)
    for j in range(half):
        keep_ref[j] = joined_ref[place_ref[level + 1] * half + j]
        send_ref[j] = joined_ref[(1 - place_ref[level + 1]) * half + j]


def crest_kernel(level, place_ref, own_ref, came_ref, early_ref, send_ref):
    second = place_ref[level] == 1
    for j in range(own_ref.shape[0]):
        own, came = own_ref[j], came_ref[j]
        early = jnp.where(second, came, own)
        early_ref[j] = early
        late = jnp.where(second, own, came)
        send_ref[j] = follow(late, early[:, HEAD_SIZE:]).astype(BF16)


def turn_kernel(level, place_ref, early_ref, came_ref, keep_ref, send_ref):
    second, later = place_ref[level] == 1, place_ref[level + 1] == 1
    for j in range(early_ref.shape[0]):
        came = came_ref[j]
        state = jnp.where(later, came, jnp.zeros_like(came))
        after = follow(early_ref[j], state).astype(BF16)
        keep_ref[j] = jnp.where(second, after, state)
        send_ref[j] = jnp.where(second, state, after)


def pass_kernel(level, place_ref, early_ref, own_ref, came_ref, keep_ref, send_ref, state_ref):
    second = place_ref[level] == 1
    half = own_ref.shape[0]
    for j in range(half):
        state_ref[place_ref[level + 1] * half + j] = own_ref[j]
        state_ref[(1 - place_ref[level + 1]) * half + j] = came_ref[j]
    for j in range(2 * half):
        state = state_ref[j]
        after = follow(early_ref[j], state).astype(BF16)
        keep_ref[j] = jnp.where(second, after, state)
        send_ref[j] = jnp.where(second, state, after)


def gate_heads(through_ref, settled_ref, gate_ref, state_ref, gain_ref, gated_ref):
    gain = gain_ref[...]
    for h in range(state_ref.shape[0]):
        lanes = slice(h * HEAD_SIZE, (h + 1) * HEAD_SIZE)
        attended = settled_ref[:, lanes] + mm(through_ref[:, lanes], state_ref[h])
        scale = lax.rsqrt(jnp.mean(attended * attended, axis=1, keepdims=True) + 1e-05)
        gate = jax.nn.sigmoid(gate_ref[:, lanes].astype(F32))
        gated_ref[:, lanes] = (attended * scale * gain * gate).astype(BF16)


def tile_spans(model):
    tile = model // 3 if model % 768 == 0 else model
    return [slice(n, n + tile) for n in range(0, model, tile)]


def part_spans(model):
    tiles = tile_spans(model)
    return [tiles[:1], tiles[1:]] if len(tiles) > 1 else [tiles]


def load_kernel(chips, place_ref, *refs):
    count = (len(refs) - 1) // 3
    sources, targets, sems = refs[:count], refs[count:-1], refs[-1]
    core, side = place_ref[0], place_ref[1]
    waits = []

    def load(source, target):
        copy = pltpu.make_async_copy(source, target, sems.at[len(waits)])
        copy.start()
        waits.append(copy)

    for n, source in enumerate(sources):
        for rest in range(2):
            target = targets[2 * n + rest]
            group = 1 - side if rest else side
            if source.shape[1] == 2 * target.shape[1]:
                span = target.shape[1]
                columns = pl.ds(pl.multiple_of(group * span, span), span)
                block = source.shape[0] // (2 * chips)
                for own in range(2):
                    for chip in range(chips):
                        first = (2 * chip + (core if own else 1 - core)) * block
                        load(
                            source.at[pl.ds(pl.multiple_of(first, block), block), columns],
                            target.at[pl.ds((own * chips + chip) * block, block)],
                        )
            else:
                span = target.shape[0]
                load(source.at[pl.ds(pl.multiple_of(group * span, span), span)], target)
    for copy in waits:
        copy.wait()


def early_kernel(
    through_ref, settled_ref, gate_ref, weight_ref, state_ref, gain_ref, total_ref, gated_ref
):
    gate_heads(through_ref, settled_ref, gate_ref, state_ref, gain_ref, gated_ref)
    for tile in tile_spans(weight_ref.shape[1]):
        total_ref[:, tile] = jnp.dot(
            gated_ref[...], weight_ref[:, tile], preferred_element_type=F32
        )


def late_kernel(
    through_ref, settled_ref, gate_ref, weight_ref, total_ref, state_ref, gain_ref, *refs
):
    targets, gated_ref = refs[:-1], refs[-1]
    chips, block = targets[0].shape[:2]
    gate_heads(through_ref, settled_ref, gate_ref, state_ref, gain_ref, gated_ref)
    for n, tiles in enumerate(part_spans(weight_ref.shape[1])):
        for tile in tiles:
            product = total_ref[:, tile] + jnp.dot(
                gated_ref[...], weight_ref[:, tile], preferred_element_type=F32
            )
            columns = slice(tile.start - tiles[0].start, tile.stop - tiles[0].start)
            for own in range(2):
                for chip in range(chips):
                    first = (own * chips + chip) * block
                    targets[2 * n + own][chip, :, columns] = product[
                        first : first + block
                    ].astype(BF16)


def in_hbm(*arrays):
    return [pltpu.with_memory_space_constraint(a, pltpu.HBM) for a in arrays]


def make_maps(operands, first, pairs, previous):
    rows, width = operands[0].shape
    heads = operands[4].shape[0]
    chunks = rows // CHUNK
    lanes = BATCH * HEAD_SIZE
    column = pl.BlockSpec((rows, lanes), lambda s, p: (0, p[0] + s))
    share = pairs * BATCH * chunks
    return pl.pallas_call(
        maps_kernel,
        grid_spec=pltpu.PrefetchScalarGridSpec(
            num_scalar_prefetch=1,
            grid=(pairs,),
            in_specs=[column] * 4
            + [pl.BlockSpec((heads, rows), lambda s, p: (0, 0))]
            + [pl.BlockSpec(memory_space=pltpu.HBM)] * len(previous),
            out_specs=[
                pl.BlockSpec((BATCH, HEAD_SIZE, 2 * HEAD_SIZE), lambda s, p: (s, 0, 0)),
                column,
                column,
            ],
        ),
        out_shape=[
            jax.ShapeDtypeStruct((BATCH * pairs, HEAD_SIZE, 2 * HEAD_SIZE), BF16),
            pltpu.HBM((rows, width), BF16),
            pltpu.HBM((rows, width), F32),
        ],
        input_output_aliases={6 + n: 1 + n for n in range(len(previous))},
        cost_estimate=pl.CostEstimate(
            flops=share * 120_000_000, bytes_accessed=share * 400_000, transcendentals=0
        ),
        compiler_params=pltpu.CompilerParams(vmem_limit_bytes=LIMIT << 20),
    )(first, *operands, *previous)


def load_halves(places, arrays, groups):
    chips = groups // 2
    hbm = pl.BlockSpec(memory_space=pltpu.HBM)
    shapes, copies = [], 0
    for array, by_rows in arrays:
        rows, width = array.shape
        shape = (rows // 2, width) if by_rows else (rows, width // 2)
        shapes += [pltpu.VMEM(shape, array.dtype)] * 2
        copies += 2 if by_rows else 4 * chips
    return pl.pallas_call(
        functools.partial(load_kernel, chips),
        in_specs=[pl.BlockSpec(memory_space=pltpu.SMEM)] + [hbm] * len(arrays),
        out_specs=[pl.BlockSpec(memory_space=pltpu.VMEM)] * len(shapes),
        out_shape=shapes,
        scratch_shapes=[pltpu.SemaphoreType.DMA((copies,))],
        cost_estimate=pl.CostEstimate(
            flops=0, bytes_accessed=10_000_000, transcendentals=0
        ),
        compiler_params=pltpu.CompilerParams(vmem_limit_bytes=LIMIT << 20),
    )(places, *in_hbm(*(array for array, _ in arrays)))


def project(through, settled, gates, weights, states, gain, groups):
    rows, span = through[0].shape
    model = weights[0].shape[1]
    chips = groups // 2
    block = rows // groups
    vmem = pl.BlockSpec(memory_space=pltpu.VMEM)
    keep, came = states
    gain = gain.reshape(1, HEAD_SIZE)
    grant = pltpu.CompilerParams(vmem_limit_bytes=LIMIT << 20)
    cost = pl.CostEstimate(
        flops=2 * rows * span * model, bytes_accessed=2 * span * model, transcendentals=0
    )
    total = pl.pallas_call(
        early_kernel,
        in_specs=[vmem] * 6,
        out_specs=vmem,
        out_shape=pltpu.VMEM((rows, model), F32),
        scratch_shapes=[pltpu.VMEM((rows, span), BF16)],
        cost_estimate=cost,
        compiler_params=grant,
        name="early",
    )(through[0], settled[0], gates[0], weights[0], keep, gain)
    widths = [tiles[-1].stop - tiles[0].start for tiles in part_spans(model)]
    shares = pl.pallas_call(
        late_kernel,
        in_specs=[vmem] * 7,
        out_specs=[vmem] * (2 * len(widths)),
        out_shape=[jax.ShapeDtypeStruct((chips, block, w), BF16) for w in widths for _ in range(2)],
        scratch_shapes=[pltpu.VMEM((rows, span), BF16)],
        cost_estimate=cost,
        compiler_params=grant,
        name="late",
    )(through[1], settled[1], gates[1], weights[1], total, came, gain)
    return list(zip(shares[::2], shares[1::2]))


def small_call(kernel, place, operands, shapes, scratch):
    def block(shape):
        return pl.BlockSpec(shape, lambda n, p: (0,) * len(shape))

    return pl.pallas_call(
        kernel,
        grid_spec=pltpu.PrefetchScalarGridSpec(
            num_scalar_prefetch=1,
            grid=(1,),
            in_specs=[block(a.shape) for a in operands],
            out_specs=[block(shape) for shape in shapes],
            scratch_shapes=[pltpu.VMEM(shape, BF16) for shape in scratch],
        ),
        out_shape=[jax.ShapeDtypeStruct(shape, BF16) for shape in shapes],
        compiler_params=pltpu.CompilerParams(vmem_limit_bytes=8 << 20),
    )(place, *operands)


def carry_apart(operands, place, axis):
    count = lax.axis_size(axis)
    heads = operands[4].shape[0]
    bits = [lax.rem(lax.div(place, 1 << n), 2) for n in range(3)]
    place_at = jnp.stack(bits).astype(jnp.int32)
    half, quarter = heads // 2, heads // 4
    batches = half // BATCH

    def swap(block, step):
        return lax.ppermute(block, axis, [(d, d ^ step) for d in range(count)])

    def first(group):
        return jnp.reshape(group * batches, (1,)).astype(jnp.int32)

    item, square = (HEAD_SIZE, 2 * HEAD_SIZE), (HEAD_SIZE, HEAD_SIZE)
    far = make_maps(operands, first(1 - bits[0]), batches, [])
    came = swap(far[0], 1)
    near = make_maps(operands, first(bits[0]), batches, far[1:])
    early, keep, send = small_call(
        functools.partial(join_kernel, 0),
        place_at,
        [near[0], came],
        [(half, *item), (quarter, *item), (quarter, *item)],
        [(half, *item)],
    )
    came = swap(send, 2)
    crest, send = small_call(
        functools.partial(crest_kernel, 1),
        place_at,
        [keep, came],
        [(quarter, *item), (quarter, *square)],
        [],
    )
    came = swap(send, 4)
    keep, send = small_call(
        functools.partial(turn_kernel, 1), place_at, [crest, came], [(quarter, *square)] * 2, []
    )
    came = swap(send, 2)
    keep, send = small_call(
        functools.partial(pass_kernel, 0),
        place_at,
        [early, keep, came],
        [(half, *square)] * 2,
        [(half, *square)],
    )
    return near[1:], [keep, swap(send, 1)], bits[0]


def carry_whole(operands, axis):
    heads = operands[4].shape[0]
    made = make_maps(operands, jnp.zeros((1,), jnp.int32), heads // BATCH, [])
    gathered = lax.all_gather(made[0], axis)

    def one(turn, state):
        item = lax.dynamic_index_in_dim(gathered, turn, 0, False).astype(F32)
        moved = jnp.einsum(
            "hij,hjk->hik", item[..., :HEAD_SIZE], state, precision=lax.Precision.HIGHEST
        )
        return moved + item[..., HEAD_SIZE:]

    zero = jnp.zeros((heads, HEAD_SIZE, HEAD_SIZE), F32)
    state = lax.fori_loop(0, lax.axis_index(axis), one, zero)
    return made[1:], jnp.split(state.astype(BF16), 2), 0


def sum_heads(other, mine, chip, groups):
    chips = groups // 2
    came = lax.ppermute(other, "head", [(d, d ^ 1) for d in range(groups)])

    def both(block):
        return lax.dynamic_index_in_dim(mine, block, 0, False).astype(
            F32
        ) + lax.dynamic_index_in_dim(came, block, 0, False).astype(F32)

    total = both(chip)
    for turn in range(1, chips):
        away = both(lax.rem(chip + turn, chips)).astype(BF16)
        hops = [(d, (d + 2 * turn) % groups) for d in range(groups)]
        total = total + lax.ppermute(away, "head", hops).astype(F32)
    return total.astype(BF16)


def on_device(
    query_vectors,
    key_vectors,
    value_vectors,
    log_decay,
    write_rate,
    out_gate,
    norm_gain,
    out_weight,
):
    heads = query_vectors.shape[1] // HEAD_SIZE
    operands = in_hbm(query_vectors, key_vectors, value_vectors, log_decay, write_rate.T)
    count = lax.axis_size("ctx")
    if count == 8 and heads == 8:
        reads, states, twist = carry_apart(operands, lax.axis_index("ctx"), "ctx")
    else:
        reads, states, twist = carry_whole(operands, "ctx")
    groups = lax.axis_size("head")
    place = lax.axis_index("head")
    core, chip = lax.rem(place, 2), lax.div(place, 2)

    places = jnp.stack([core, jnp.asarray(twist, core.dtype)]).astype(jnp.int32)
    loaded = load_halves(places, [(out_weight, True), (out_gate, False)], groups)
    weights, gates = loaded[:2], loaded[2:]
    loaded = load_halves(places, [(reads[0], False), (reads[1], False)], groups)
    shares = project(loaded[:2], loaded[2:], gates, weights, states, norm_gain, groups)
    sums = [sum_heads(*share, chip, groups) for share in shares]
    return jnp.concatenate(sums, axis=1)


def solution(mesh):
    in_specs = (
        P("ctx", "head"),
        P("ctx", "head"),
        P("ctx", "head"),
        P("ctx", "head"),
        P("ctx", "head"),
        P("ctx", "head"),
        P(),
        P("head", None),
    )
    out_specs = P(("ctx", "head"), None)

    return jax.shard_map(
        on_device, mesh=mesh, in_specs=in_specs, out_specs=out_specs, check_vma=False
    )
```
